128 devices in a mesh: req: 16 (over z, y), kv: 8 (over x, core).
Axes of the slice: x: 4, y: 4, z: 4, core: 2. Of those that a mesh axis runs over, the one named last changes fastest.
Arguments:
- hidden_in: bfloat16 [16384, 2048], P(('req', 'kv')), may hold values from -6 to 6
- slot_tokens: int32 [16384], replicated, may hold values from 0 to 16383, as said below
- cache_len: int32 [128], P('req'), may hold values from 1 to 2048, 65536 in all
- prefill_start: int32 [16], P('req'), may hold values from 0 to 2048
- key_cache: bfloat16 [128, 2048, 1024], P('req', None, 'kv')
- value_cache: bfloat16 [128, 2048, 1024], P('req', None, 'kv'), may hold values from -18 to 18
- key_prefix: bfloat16 [16, 2048, 1024], P('req', None, 'kv')
- value_prefix: bfloat16 [16, 2048, 1024], P('req', None, 'kv'), may hold values from -18 to 18
- attn_gain: float32 [2048], replicated, may hold values from 0.25 to 1.75
- q_proj: bfloat16 [2048, 2048], P(None, 'kv'), may hold values from -0.125 to 0.125
- k_proj: bfloat16 [2048, 1024], P(None, 'kv'), may hold values from -0.125 to 0.125
- v_proj: bfloat16 [2048, 1024], P(None, 'kv'), may hold values from -0.125 to 0.125
- q_gain: float32 [128], replicated, may hold values from 0.25 to 1.75
- k_gain: float32 [128], replicated, may hold values from 0.25 to 1.75
- o_proj: bfloat16 [2048, 2048], P('kv'), may hold values from -0.125 to 0.125
- ffn_gain: float32 [2048], replicated, may hold values from 0.25 to 1.75
- w_gate: bfloat16 [2048, 6144], P(None, 'req'), may hold values from -0.125 to 0.125
- w_up: bfloat16 [2048, 6144], P(None, 'req'), may hold values from -0.125 to 0.125
- w_down: bfloat16 [6144, 2048], P('req'), may hold values from -0.078125 to 0.078125
- final_gain: float32 [2048], replicated, may hold values from 0.25 to 1.75
- lm_head: bfloat16 [2048, 151936], P(None, ('req', 'kv')), may hold values from -0.375 to 0.375
Outputs:
- layer_out: bfloat16 [16384, 2048], P(('req', 'kv'))
- max_logit: float32 [144], replicated
The draws below stay inside these ranges and needn't reach their ends.
Inputs may be any that keep to these rules, and one draw needn't show every extreme that they name: slot_tokens is a permutation of the batch's tokens; each device's 128 consecutive slots take exactly 1 token from each device's 128 consecutive batch tokens.
All inputs are finite; a program needn't handle non-finite values. No bound on the sum of `cache_len` on one device may be relied on, other than what follows from the above.
Results may differ from the reference program's by a relative error of at most 0.0085.
The reference program's roundings to bfloat16 on the way count: a program that leaves them out, or rounds other values in their place, can miss the bound.
Values may be sent and summed in bfloat16 or wider, within the bound.
A program may use at most 128 MiB of HBM per device.

```python
import math
import jax
import jax.numpy as jnp
import numpy as np
from jax import lax

D = 2048
HEADS = 16
KV_HEADS = 8
HEAD_DIM = 128
FF = 6144
VOCAB = 151936
DEC_DEV = 8
TOK_REQ = 1024
CACHE = 2048
PREFIX = 2048
PREFILL_TOK = 1016
ROWS = 128
TOKENS = 16384
DEC = 128
LOGIT_ROWS = 144
N_REQ = 16


def draw_slot_tokens(key, part):
    devices = TOKENS // ROWS
    per_pair = ROWS // devices
    first_keys = jax.random.split(jax.random.fold_in(key, 11), devices)
    shuffled = jax.vmap(lambda sub_key: jax.random.permutation(sub_key, ROWS))(first_keys).astype(jnp.int32)
    tokens_by = shuffled + (jnp.arange(devices, dtype=jnp.int32) * ROWS)[:, None]
    grouped = tokens_by.reshape(devices, devices, per_pair).transpose(1, 0, 2).reshape(devices, ROWS)
    second_keys = jax.random.split(jax.random.fold_in(key, 12), devices)
    orders = jax.vmap(lambda sub_key: jax.random.permutation(sub_key, ROWS))(second_keys).astype(jnp.int32)
    return jnp.take_along_axis(grouped, orders, axis=1).reshape(TOKENS).astype(jnp.int32)


def draw_prefill_start(key, part):
    base_draw = jax.random.randint(jax.random.fold_in(key, 21), (N_REQ,), 0, PREFIX + 1).astype(jnp.int32)
    skewed = base_draw * base_draw // PREFIX
    chosen = jax.random.randint(jax.random.fold_in(key, 22), (), 0, N_REQ)
    return skewed.at[chosen].set(PREFIX).astype(jnp.int32)


def shifted_keys(key, lead, slots):
    shape = (lead, slots, KV_HEADS, HEAD_DIM)
    noise = 3.0 * jnp.clip(jax.random.normal(key, shape, jnp.float32), -6.0, 6.0)
    offset = 40.0 * float(HEAD_DIM) ** 0.5
    lift = jnp.where(jnp.arange(HEAD_DIM, dtype=jnp.int32) == 0, offset, 0.0).astype(jnp.float32)
    return (noise + lift).reshape(lead, slots, KV_HEADS * HEAD_DIM).astype(jnp.bfloat16)


def draw_key_cache(key, part):
    return shifted_keys(jax.random.fold_in(key, 31), DEC, CACHE)


def draw_key_prefix(key, part):
    return shifted_keys(jax.random.fold_in(key, 32), N_REQ, PREFIX)


def block_levels(key, shape, shards, low, top_value):
    level = 1.0
    for axis_at, blocks in shards:
        steps = jax.random.uniform(jax.random.fold_in(jax.random.fold_in(key, 6), axis_at), (blocks,), jnp.float32, low / len(shards), top_value / len(shards))
        level = level * jnp.repeat(jnp.exp(steps), shape[axis_at] // blocks).reshape((-1,) + (1,) * (len(shape) - 1 - axis_at))
    return level


def split_up(number_of, total, reach, slope):
    weights = [(1 << 20) // math.isqrt(standing ** slope) + 1 for standing in range(2, number_of + 1)]
    spare, counts = total - reach - (number_of - 1), [1] * (number_of - 1)
    while spare > 0:
        movable = [i for i in range(number_of - 1) if counts[i] < reach]
        pool, left = sum([weights[i] for i in movable]), spare
        for i in movable:
            addition = min(reach - counts[i], max(1, left * weights[i] // pool), spare)
            counts[i] = counts[i] + addition
            spare = spare - addition
    return np.array([reach] + counts)


def ragged_sizes(own_key, count, total, most, lean):
    if count == 2:
        one = jax.random.randint(own_key, (), max(1, total - most), min(most, total - 1) + 1)
        return jnp.stack([one, total - one])
    sizes = jnp.asarray(split_up(count, total, most, lean), jnp.int32)
    twos = (count - 1) // 2
    source_of, receiver = sizes[1:1 + 2 * twos:2], sizes[2:2 + 2 * twos:2]
    margin = jnp.minimum(source_of - 1, most - receiver)
    shifted = jax.random.randint(jax.random.fold_in(own_key, 1), (twos,), 0, 1 << 20) % (margin + 1)
    sizes = sizes.at[1:1 + 2 * twos:2].set(source_of - shifted).at[2:2 + 2 * twos:2].set(receiver + shifted)
    return sizes[jax.random.permutation(jax.random.fold_in(own_key, 2), count)]


def centred(stream_key, dims, spread, reach, cuts=(), kind=jnp.bfloat16):
    entries = spread * jax.random.normal(stream_key, dims, jnp.float32)
    if cuts:
        entries = entries * block_levels(stream_key, dims, cuts, -0.22, 0.18)
    return jnp.clip(entries, -reach, reach).astype(kind)


def setup_inputs(seed: int = 0) -> dict:
    streams_of = jax.random.split(jax.random.key(seed), 22)
    hidden_in = centred(streams_of[0], (TOKENS, D), 1.0, 6.0, ((0, 128),))
    slot_tokens = draw_slot_tokens(jax.random.fold_in(streams_of[21], 71), 0)
    cache_len = ragged_sizes(streams_of[2], DEC, DEC * CACHE // 4, CACHE, 2).astype(jnp.int32)
    prefill_start = draw_prefill_start(jax.random.fold_in(streams_of[21], 71), 0)
    key_cache = draw_key_cache(jax.random.fold_in(streams_of[21], 71), 0)
    value_cache = centred(streams_of[5], (DEC, CACHE, KV_HEADS * HEAD_DIM), 3.0, 18.0, ((0, 16), (2, 8)))
    key_prefix = draw_key_prefix(jax.random.fold_in(streams_of[21], 71), 0)
    value_prefix = centred(streams_of[7], (N_REQ, PREFIX, KV_HEADS * HEAD_DIM), 3.0, 18.0, ((0, 16), (2, 8)))
    attn_gain = jnp.clip(1.0 + 0.15 * jax.random.normal(streams_of[8], (D,), jnp.float32), 0.25, 1.75)
    q_proj = centred(streams_of[9], (D, HEADS * HEAD_DIM), D ** -0.5, 0.125, ((1, 8),))
    k_proj = centred(streams_of[10], (D, KV_HEADS * HEAD_DIM), D ** -0.5, 0.125, ((1, 8),))
    v_proj = centred(streams_of[11], (D, KV_HEADS * HEAD_DIM), D ** -0.5, 0.125, ((1, 8),))
    q_gain = jnp.clip(1.0 + 0.15 * jax.random.normal(streams_of[12], (HEAD_DIM,), jnp.float32), 0.25, 1.75)
    k_gain = jnp.clip(1.0 + 0.15 * jax.random.normal(streams_of[13], (HEAD_DIM,), jnp.float32), 0.25, 1.75)
    o_proj = centred(streams_of[14], (HEADS * HEAD_DIM, D), (HEADS * HEAD_DIM) ** -0.5, 0.125, ((0, 8),))
    ffn_gain = jnp.clip(1.0 + 0.15 * jax.random.normal(streams_of[15], (D,), jnp.float32), 0.25, 1.75)
    w_gate = centred(streams_of[16], (D, FF), D ** -0.5, 0.125, ((1, 16),))
    w_up = centred(streams_of[17], (D, FF), D ** -0.5, 0.125, ((1, 16),))
    w_down = centred(streams_of[18], (FF, D), FF ** -0.5, 0.078125, ((0, 16),))
    final_gain = jnp.clip(1.0 + 0.15 * jax.random.normal(streams_of[19], (D,), jnp.float32), 0.25, 1.75)
    lm_head = centred(streams_of[20], (D, VOCAB), (D // 9) ** -0.5, 0.375, ((1, 128),))
    return {"hidden_in": hidden_in, "slot_tokens": slot_tokens, "cache_len": cache_len, "prefill_start": prefill_start, "key_cache": key_cache, "value_cache": value_cache, "key_prefix": key_prefix, "value_prefix": value_prefix, "attn_gain": attn_gain, "q_proj": q_proj, "k_proj": k_proj, "v_proj": v_proj, "q_gain": q_gain, "k_gain": k_gain, "o_proj": o_proj, "ffn_gain": ffn_gain, "w_gate": w_gate, "w_up": w_up, "w_down": w_down, "final_gain": final_gain, "lm_head": lm_head}


EPS = 1e-06
NEG = -1e+30

def norm_rows(values, gain_vec):
    wide = values.astype(jnp.float32)
    return wide * lax.rsqrt(lax.optimization_barrier(jnp.mean(wide * wide, axis=-1, keepdims=True)) + EPS) * gain_vec

def rotate(values, places):
    half_dim = values.shape[-1] // 2
    freqs = 1000000.0 ** (-(jnp.arange(half_dim, dtype=jnp.float32) * 2.0 / values.shape[-1]))
    angles = places[:, None] * freqs[None, :]
    cosine = jnp.cos(angles)[:, None, :]
    sine = jnp.sin(angles)[:, None, :]
    first_half = values[..., :half_dim]
    second_half = values[..., half_dim:]
    return jnp.concatenate([first_half * cosine - second_half * sine, second_half * cosine + first_half * sine], axis=-1)

def prefill_attend(q_heads, key_old, value_old, key_new, value_new, start_at):
    old_len = key_old.shape[0]
    fresh_rows = q_heads.shape[0]
    factor = q_heads.shape[-1] ** (-0.5)
    all_keys = jnp.concatenate([key_old, key_new], axis=0).astype(jnp.float32)
    all_values = jnp.concatenate([value_old, value_new], axis=0).astype(jnp.float32)
    scores = jnp.einsum('cgd,kd->gck', q_heads.astype(jnp.float32), all_keys) * factor
    key_index = jnp.arange(old_len + fresh_rows, dtype=jnp.int32)[None, :]
    row_index = jnp.arange(fresh_rows, dtype=jnp.int32)[:, None]
    allowed = jnp.where(key_index < old_len, key_index < start_at, key_index - old_len <= row_index)
    scores = jnp.where(allowed[None], scores, NEG)
    row_peak = lax.optimization_barrier(jnp.max(scores, axis=-1, keepdims=True))
    expd = jnp.exp(scores - row_peak)
    weights = (expd / lax.optimization_barrier(jnp.sum(expd, axis=-1, keepdims=True))).astype(jnp.bfloat16)
    return jnp.einsum('gck,kd->cgd', weights.astype(jnp.float32), all_values).astype(jnp.bfloat16)

def decode_attend(q_heads, key_old, value_old, key_self, value_self, lengths):
    factor = q_heads.shape[-1] ** (-0.5)
    past = jnp.einsum('bgd,bld->bgl', q_heads.astype(jnp.float32), key_old.astype(jnp.float32)) * factor
    slot_index = jnp.arange(key_old.shape[1], dtype=jnp.int32)
    past = jnp.where(slot_index[None, None, :] < lengths[:, None, None], past, NEG)
    own_score = jnp.einsum('bgd,bd->bg', q_heads.astype(jnp.float32), key_self.astype(jnp.float32)) * factor
    row_peak = jnp.maximum(lax.optimization_barrier(jnp.max(past, axis=-1)), own_score)
    past_exp = jnp.exp(past - row_peak[..., None])
    own_exp = jnp.exp(own_score - row_peak)
    row_total = lax.optimization_barrier(jnp.sum(past_exp, axis=-1)) + own_exp
    past_w = (past_exp / row_total[..., None]).astype(jnp.bfloat16)
    own_w = (own_exp / row_total).astype(jnp.bfloat16)
    summed = jnp.einsum('bgl,bld->bgd', past_w.astype(jnp.float32), value_old.astype(jnp.float32))
    summed = summed + own_w.astype(jnp.float32)[..., None] * value_self.astype(jnp.float32)[:, None, :]
    return summed.astype(jnp.bfloat16)

def reference(hidden_in, slot_tokens, cache_len, prefill_start, key_cache, value_cache, key_prefix, value_prefix, attn_gain, q_proj, k_proj, v_proj, q_gain, k_gain, o_proj, ffn_gain, w_gate, w_up, w_down, final_gain, lm_head):
    owner_rows = hidden_in[slot_tokens]
    normed = norm_rows(owner_rows, attn_gain).astype(jnp.bfloat16)
    q_raw = jnp.dot(normed, q_proj, preferred_element_type=jnp.float32).reshape(TOKENS, HEADS, HEAD_DIM)
    k_raw = jnp.dot(normed, k_proj, preferred_element_type=jnp.float32).reshape(TOKENS, KV_HEADS, HEAD_DIM)
    v_new = jnp.dot(normed, v_proj, preferred_element_type=jnp.float32).astype(jnp.bfloat16).reshape(N_REQ, TOK_REQ, KV_HEADS, HEAD_DIM)
    fresh_pos = prefill_start[:, None] + jnp.arange(PREFILL_TOK, dtype=jnp.int32)[None, :]
    places = jnp.concatenate([fresh_pos, cache_len.reshape(N_REQ, DEC_DEV)], axis=1).astype(jnp.float32).reshape(TOKENS)
    queries = rotate(norm_rows(q_raw, q_gain), places).astype(jnp.bfloat16).reshape(N_REQ, TOK_REQ, HEADS, HEAD_DIM)
    keys_new = rotate(norm_rows(k_raw, k_gain), places).astype(jnp.bfloat16).reshape(N_REQ, TOK_REQ, KV_HEADS, HEAD_DIM)
    group_size = HEADS // KV_HEADS
    dec_keys = key_cache.reshape(N_REQ, DEC_DEV, CACHE, KV_HEADS * HEAD_DIM)
    dec_values = value_cache.reshape(N_REQ, DEC_DEV, CACHE, KV_HEADS * HEAD_DIM)
    dec_lengths = cache_len.reshape(N_REQ, DEC_DEV)

    def one_owner(inputs):
        q_own, k_own, v_own, key_dec, value_dec, key_pre, value_pre, lengths, start_at = inputs
        pieces = []
        for head_id in range(KV_HEADS):
            cols = slice(head_id * HEAD_DIM, (head_id + 1) * HEAD_DIM)
            q_group = q_own[:, head_id * group_size:(head_id + 1) * group_size]
            pre_out = prefill_attend(q_group[:PREFILL_TOK], key_pre[:, cols], value_pre[:, cols], k_own[:PREFILL_TOK, head_id], v_own[:PREFILL_TOK, head_id], start_at)
            dec_out = decode_attend(q_group[PREFILL_TOK:], key_dec[:, :, cols], value_dec[:, :, cols], k_own[PREFILL_TOK:, head_id], v_own[PREFILL_TOK:, head_id], lengths)
            pieces.append(jnp.concatenate([pre_out, dec_out], axis=0))
        return jnp.concatenate(pieces, axis=1).reshape(TOK_REQ, HEADS * HEAD_DIM)
    attended = lax.map(one_owner, (queries, keys_new, v_new, dec_keys, dec_values, key_prefix, value_prefix, dec_lengths, prefill_start))
    attended = attended.reshape(TOKENS, HEADS * HEAD_DIM)
    resid = (owner_rows.astype(jnp.float32) + jnp.dot(attended, o_proj, preferred_element_type=jnp.float32)).astype(jnp.bfloat16)
    ffn_in = norm_rows(resid, ffn_gain).astype(jnp.bfloat16)

    def ffn_block(rows_block):
        gate_part = jnp.dot(rows_block, w_gate, preferred_element_type=jnp.float32)
        up_part = jnp.dot(rows_block, w_up, preferred_element_type=jnp.float32)
        hidden_act = (jax.nn.silu(gate_part) * up_part).astype(jnp.bfloat16)
        return jnp.dot(hidden_act, w_down, preferred_element_type=jnp.float32)
    ffn_part = lax.map(ffn_block, ffn_in.reshape(N_REQ, TOK_REQ, D)).reshape(TOKENS, D)
    out_rows = (resid.astype(jnp.float32) + ffn_part).astype(jnp.bfloat16)
    layer_out = jnp.zeros_like(hidden_in).at[slot_tokens].set(out_rows)
    tail_rows = out_rows.reshape(N_REQ, TOK_REQ, D)[:, PREFILL_TOK - 1:].reshape(LOGIT_ROWS, D)
    tail_rows = norm_rows(tail_rows, final_gain).astype(jnp.bfloat16)
    logits = jnp.dot(tail_rows, lm_head, preferred_element_type=jnp.float32)
    max_logit = lax.optimization_barrier(jnp.max(logits, axis=1))
    return (layer_out, max_logit)
```

```python
import jax
import jax.numpy as jnp
from jax import lax
from jax.sharding import PartitionSpec as P

EPS = 1e-06
NEG = -1e30


def spread(value, axis, root):
    mine = lax.axis_index(axis) == root
    return lax.psum(jnp.where(mine, value, jnp.zeros_like(value)), axis)


def norm_rows(values, gain_vec):
    wide = values.astype(jnp.float32)
    return wide * lax.rsqrt(jnp.mean(wide * wide, axis=-1, keepdims=True) + EPS) * gain_vec


def rotate(values, places):
    half_dim = values.shape[-1] // 2
    freqs = 1000000.0 ** (-(jnp.arange(half_dim, dtype=jnp.float32) * 2.0 / values.shape[-1]))
    angles = places[:, None] * freqs[None, :]
    cosine = jnp.cos(angles)[:, None, :]
    sine = jnp.sin(angles)[:, None, :]
    first_half = values[..., :half_dim]
    second_half = values[..., half_dim:]
    return jnp.concatenate(
        [first_half * cosine - second_half * sine, second_half * cosine + first_half * sine],
        axis=-1,
    )


def prefill_full(q_heads, key_old, value_old, key_new, value_new, start_at):
    old_len = key_old.shape[0]
    fresh_rows = q_heads.shape[0]
    factor = q_heads.shape[-1] ** (-0.5)
    all_keys = jnp.concatenate([key_old, key_new], axis=0)
    all_values = jnp.concatenate([value_old, value_new], axis=0)
    scores = (
        jnp.einsum("cgd,kd->gck", q_heads, all_keys, preferred_element_type=jnp.float32) * factor
    )
    key_index = jnp.arange(old_len + fresh_rows, dtype=jnp.int32)[None, :]
    row_index = jnp.arange(fresh_rows, dtype=jnp.int32)[:, None]
    allowed = jnp.where(key_index < old_len, key_index < start_at, key_index - old_len <= row_index)
    scores = jnp.where(allowed[None], scores, NEG)
    row_peak = jnp.max(scores, axis=-1, keepdims=True)
    expd = jnp.exp(scores - row_peak)
    weights = (expd / jnp.sum(expd, axis=-1, keepdims=True)).astype(jnp.bfloat16)
    return jnp.einsum(
        "gck,kd->cgd", weights, all_values, preferred_element_type=jnp.float32
    ).astype(jnp.bfloat16)


def decode_attend(q_heads, key_old, value_old, key_self, value_self, lengths):
    factor = q_heads.shape[-1] ** (-0.5)
    past = jnp.einsum("bgd,bld->bgl", q_heads, key_old, preferred_element_type=jnp.float32) * factor
    slot_index = jnp.arange(key_old.shape[1], dtype=jnp.int32)
    past = jnp.where(slot_index[None, None, :] < lengths[:, None, None], past, NEG)
    own_score = (
        jnp.einsum("bgd,bd->bg", q_heads, key_self, preferred_element_type=jnp.float32) * factor
    )
    row_peak = jnp.maximum(jnp.max(past, axis=-1), own_score)
    past_exp = jnp.exp(past - row_peak[..., None])
    own_exp = jnp.exp(own_score - row_peak)
    row_total = jnp.sum(past_exp, axis=-1) + own_exp
    past_w = (past_exp / row_total[..., None]).astype(jnp.bfloat16)
    own_w = (own_exp / row_total).astype(jnp.bfloat16)
    summed = jnp.einsum("bgl,bld->bgd", past_w, value_old, preferred_element_type=jnp.float32)
    summed = (
        summed + own_w.astype(jnp.float32)[..., None] * value_self.astype(jnp.float32)[:, None, :]
    )
    return summed.astype(jnp.bfloat16)


def regroup(rows_in):
    return lax.all_to_all(rows_in, ("req", "kv"), split_axis=0, concat_axis=0, tiled=True)


def shards(
    hidden_in,
    slot_tokens,
    cache_len,
    prefill_start,
    key_cache,
    value_cache,
    key_prefix,
    value_prefix,
    attn_gain,
    q_proj,
    k_proj,
    v_proj,
    q_gain,
    k_gain,
    o_proj,
    ffn_gain,
    w_gate,
    w_up,
    w_down,
    final_gain,
    lm_head,
):
    req_count = lax.axis_size("req")
    kv_count = lax.axis_size("kv")
    devices = req_count * kv_count
    rows_dev = hidden_in.shape[0]
    kv_index = lax.axis_index("kv")
    self_index = lax.axis_index("req") * kv_count + kv_index
    slot_table = slot_tokens.reshape(devices, rows_dev)
    from_self = slot_table // rows_dev == self_index
    send_rows = jnp.sum(jnp.where(from_self, slot_table - self_index * rows_dev, 0), axis=1)
    slot_place = lax.dynamic_index_in_dim(slot_table, self_index, 0, keepdims=False) // rows_dev
    arrived = regroup(hidden_in[send_rows])
    owner_rows = arrived[slot_place]
    rows_all = lax.all_gather(owner_rows, "kv", axis=0, tiled=True)
    normed = norm_rows(rows_all, attn_gain).astype(jnp.bfloat16)
    o_full = lax.all_gather(o_proj, "kv", axis=0, tiled=True)
    ff_dev = w_gate.shape[1]
    ff_piece = ff_dev // kv_count
    gate_w = lax.all_gather(
        lax.dynamic_slice_in_dim(w_gate, kv_index * ff_piece, ff_piece, axis=1), "req", axis=1, tiled=True
    )
    up_w = lax.all_gather(
        lax.dynamic_slice_in_dim(w_up, kv_index * ff_piece, ff_piece, axis=1), "req", axis=1, tiled=True
    )
    down_w = lax.all_gather(
        lax.dynamic_slice_in_dim(w_down, kv_index * ff_piece, ff_piece, axis=0), "req", axis=0, tiled=True
    )
    q_cols = q_proj.shape[1]
    kv_cols = k_proj.shape[1]
    projected = jnp.concatenate(
        [
            jnp.dot(normed, q_proj, preferred_element_type=jnp.float32),
            jnp.dot(normed, k_proj, preferred_element_type=jnp.float32),
            jnp.dot(normed, v_proj, preferred_element_type=jnp.float32),
        ],
        axis=1,
    )
    tok_req = projected.shape[0]
    head_dim = q_gain.shape[0]
    dec_count = cache_len.shape[0]
    fresh_count = tok_req - dec_count
    q_raw = projected[:, :q_cols].reshape(tok_req, q_cols // head_dim, head_dim)
    k_raw = projected[:, q_cols : q_cols + kv_cols].reshape(tok_req, kv_cols // head_dim, head_dim)
    v_new = (
        projected[:, q_cols + kv_cols :]
        .astype(jnp.bfloat16)
        .reshape(tok_req, kv_cols // head_dim, head_dim)
    )
    places = jnp.concatenate(
        [prefill_start[0] + jnp.arange(fresh_count, dtype=jnp.int32), cache_len]
    ).astype(jnp.float32)
    queries = rotate(norm_rows(q_raw, q_gain), places).astype(jnp.bfloat16)
    keys_new = rotate(norm_rows(k_raw, k_gain), places).astype(jnp.bfloat16)
    pre_out = prefill_full(
        queries[:fresh_count],
        key_prefix[0, :, 0:head_dim],
        value_prefix[0, :, 0:head_dim],
        keys_new[:fresh_count, 0],
        v_new[:fresh_count, 0],
        prefill_start[0],
    )
    dec_out = decode_attend(
        queries[fresh_count:],
        key_cache,
        value_cache,
        keys_new[fresh_count:, 0],
        v_new[fresh_count:, 0],
        cache_len,
    )
    pieces = jnp.concatenate([pre_out, dec_out], axis=0)
    pieces, gate_w, up_w, down_w = lax.optimization_barrier((pieces, gate_w, up_w, down_w))
    attended = lax.all_gather(pieces.reshape(tok_req, q_cols), "kv", axis=1, tiled=True)
    resid = (
        rows_all.astype(jnp.float32) + jnp.dot(attended, o_full, preferred_element_type=jnp.float32)
    ).astype(jnp.bfloat16)
    ffn_in = norm_rows(resid, ffn_gain).astype(jnp.bfloat16)
    gate_part = jnp.dot(ffn_in, gate_w, preferred_element_type=jnp.float32)
    up_part = jnp.dot(ffn_in, up_w, preferred_element_type=jnp.float32)
    hidden_act = (jax.nn.silu(gate_part) * up_part).astype(jnp.bfloat16)
    down_part = jnp.dot(hidden_act, down_w, preferred_element_type=jnp.float32)
    ffn_part = lax.psum_scatter(down_part, "kv", scatter_dimension=0, tiled=True)
    mine = lax.dynamic_slice_in_dim(resid, kv_index * rows_dev, rows_dev, axis=0)
    out_rows = (mine.astype(jnp.float32) + ffn_part).astype(jnp.bfloat16)
    going_back = jnp.zeros_like(out_rows).at[slot_place].set(out_rows)
    returned = regroup(going_back)
    layer_out = jnp.zeros_like(hidden_in).at[send_rows].set(returned)
    tail_sum = lax.psum(down_part[fresh_count - 1 :], "kv")
    tail_out = (resid[fresh_count - 1 :].astype(jnp.float32) + tail_sum).astype(jnp.bfloat16)
    tail_rows = norm_rows(tail_out, final_gain).astype(jnp.bfloat16)
    local_peaks = jnp.max(
        jnp.dot(
            lax.all_gather(tail_rows, "req", axis=0, tiled=True),
            lm_head,
            preferred_element_type=jnp.float32,
        ),
        axis=1,
    )
    max_logit = lax.pmax(local_peaks, ("req", "kv"))
    return (layer_out, max_logit)


def solution(mesh):
    placed = (
        P(("req", "kv"), None),
        P(),
        P("req"),
        P("req"),
        P("req", None, "kv"),
        P("req", None, "kv"),
        P("req", None, "kv"),
        P("req", None, "kv"),
        P(),
        P(None, "kv"),
        P(None, "kv"),
        P(None, "kv"),
        P(),
        P(),
        P("kv", None),
        P(),
        P(None, "req"),
        P(None, "req"),
        P("req", None),
        P(),
        P(None, ("req", "kv")),
    )
    return jax.shard_map(
        shards, mesh=mesh, in_specs=placed, out_specs=(P(("req", "kv"), None), P()), check_vma=False
    )
```

```python
import jax
import jax.numpy as jnp
from jax import lax
from jax.sharding import PartitionSpec as P

EPS = 1e-06
NEG = -1e30


def spread(value, axis, root):
    mine = lax.axis_index(axis) == root
    return lax.psum(jnp.where(mine, value, jnp.zeros_like(value)), axis)


def norm_rows(values, gain_vec):
    wide = values.astype(jnp.float32)
    return wide * lax.rsqrt(jnp.mean(wide * wide, axis=-1, keepdims=True) + EPS) * gain_vec


def rotate(values, places):
    half_dim = values.shape[-1] // 2
    freqs = 1000000.0 ** (-(jnp.arange(half_dim, dtype=jnp.float32) * 2.0 / values.shape[-1]))
    angles = places[:, None] * freqs[None, :]
    cosine = jnp.cos(angles)[:, None, :]
    sine = jnp.sin(angles)[:, None, :]
    first_half = values[..., :half_dim]
    second_half = values[..., half_dim:]
    return jnp.concatenate(
        [first_half * cosine - second_half * sine, second_half * cosine + first_half * sine],
        axis=-1,
    )


def prefill_full(q_heads, key_old, value_old, key_new, value_new, start_at):
    old_len = key_old.shape[0]
    fresh_rows = q_heads.shape[0]
    factor = q_heads.shape[-1] ** (-0.5)
    all_keys = jnp.concatenate([key_old, key_new], axis=0)
    all_values = jnp.concatenate([value_old, value_new], axis=0)
    scores = (
        jnp.einsum("cgd,kd->gck", q_heads, all_keys, preferred_element_type=jnp.float32) * factor
    )
    key_index = jnp.arange(old_len + fresh_rows, dtype=jnp.int32)[None, :]
    row_index = jnp.arange(fresh_rows, dtype=jnp.int32)[:, None]
    allowed = jnp.where(key_index < old_len, key_index < start_at, key_index - old_len <= row_index)
    scores = jnp.where(allowed[None], scores, NEG)
    row_peak = jnp.max(scores, axis=-1, keepdims=True)
    expd = jnp.exp(scores - row_peak)
    weights = (expd / jnp.sum(expd, axis=-1, keepdims=True)).astype(jnp.bfloat16)
    return jnp.einsum(
        "gck,kd->cgd", weights, all_values, preferred_element_type=jnp.float32
    ).astype(jnp.bfloat16)


def decode_attend(q_heads, key_old, value_old, key_self, value_self, lengths):
    factor = q_heads.shape[-1] ** (-0.5)
    past = jnp.einsum("bgd,bld->bgl", q_heads, key_old, preferred_element_type=jnp.float32) * factor
    slot_index = jnp.arange(key_old.shape[1], dtype=jnp.int32)
    past = jnp.where(slot_index[None, None, :] < lengths[:, None, None], past, NEG)
    own_score = (
        jnp.einsum("bgd,bd->bg", q_heads, key_self, preferred_element_type=jnp.float32) * factor
    )
    row_peak = jnp.maximum(jnp.max(past, axis=-1), own_score)
    past_exp = jnp.exp(past - row_peak[..., None])
    own_exp = jnp.exp(own_score - row_peak)
    row_total = jnp.sum(past_exp, axis=-1) + own_exp
    past_w = (past_exp / row_total[..., None]).astype(jnp.bfloat16)
    own_w = (own_exp / row_total).astype(jnp.bfloat16)
    summed = jnp.einsum("bgl,bld->bgd", past_w, value_old, preferred_element_type=jnp.float32)
    summed = (
        summed + own_w.astype(jnp.float32)[..., None] * value_self.astype(jnp.float32)[:, None, :]
    )
    return summed.astype(jnp.bfloat16)


def regroup(rows_in):
    return lax.all_to_all(rows_in, ("req", "kv"), split_axis=0, concat_axis=0, tiled=True)


def shards(
    hidden_in,
    slot_tokens,
    cache_len,
    prefill_start,
    key_cache,
    value_cache,
    key_prefix,
    value_prefix,
    attn_gain,
    q_proj,
    k_proj,
    v_proj,
    q_gain,
    k_gain,
    o_proj,
    ffn_gain,
    w_gate,
    w_up,
    w_down,
    final_gain,
    lm_head,
):
    req_count = lax.axis_size("req")
    kv_count = lax.axis_size("kv")
    devices = req_count * kv_count
    rows_dev = hidden_in.shape[0]
    kv_index = lax.axis_index("kv")
    self_index = lax.axis_index("req") * kv_count + kv_index
    slot_table = slot_tokens.reshape(devices, rows_dev)
    from_self = slot_table // rows_dev == self_index
    send_rows = jnp.sum(jnp.where(from_self, slot_table - self_index * rows_dev, 0), axis=1)
    slot_place = lax.dynamic_index_in_dim(slot_table, self_index, 0, keepdims=False) // rows_dev
    arrived = regroup(hidden_in[send_rows])
    owner_rows = arrived[slot_place]
    rows_all = lax.all_gather(owner_rows, "kv", axis=0, tiled=True)
    normed = norm_rows(rows_all, attn_gain).astype(jnp.bfloat16)
    o_full = lax.all_gather(o_proj, "kv", axis=0, tiled=True)
    ff_dev = w_gate.shape[1]
    ff_piece = ff_dev // kv_count
    weight_piece = jnp.concatenate(
        [
            lax.dynamic_slice_in_dim(w_gate, kv_index * ff_piece, ff_piece, axis=1),
            lax.dynamic_slice_in_dim(w_up, kv_index * ff_piece, ff_piece, axis=1),
            lax.dynamic_slice_in_dim(w_down, kv_index * ff_piece, ff_piece, axis=0).T,
        ],
        axis=1,
    )
    weight_all = lax.all_to_all(
        jnp.broadcast_to(weight_piece[None], (req_count,) + weight_piece.shape),
        "req",
        split_axis=0,
        concat_axis=0,
        tiled=True,
    )
    model_dim = w_gate.shape[0]
    gate_w = weight_all[:, :, :ff_piece].transpose(1, 0, 2).reshape(model_dim, req_count * ff_piece)
    up_w = weight_all[:, :, ff_piece : 2 * ff_piece].transpose(1, 0, 2).reshape(
        model_dim, req_count * ff_piece
    )
    down_w = weight_all[:, :, 2 * ff_piece :].transpose(0, 2, 1).reshape(req_count * ff_piece, model_dim)
    q_cols = q_proj.shape[1]
    kv_cols = k_proj.shape[1]
    projected = jnp.concatenate(
        [
            jnp.dot(normed, q_proj, preferred_element_type=jnp.float32),
            jnp.dot(normed, k_proj, preferred_element_type=jnp.float32),
            jnp.dot(normed, v_proj, preferred_element_type=jnp.float32),
        ],
        axis=1,
    )
    tok_req = projected.shape[0]
    head_dim = q_gain.shape[0]
    dec_count = cache_len.shape[0]
    fresh_count = tok_req - dec_count
    q_raw = projected[:, :q_cols].reshape(tok_req, q_cols // head_dim, head_dim)
    k_raw = projected[:, q_cols : q_cols + kv_cols].reshape(tok_req, kv_cols // head_dim, head_dim)
    v_new = (
        projected[:, q_cols + kv_cols :]
        .astype(jnp.bfloat16)
        .reshape(tok_req, kv_cols // head_dim, head_dim)
    )
    places = jnp.concatenate(
        [prefill_start[0] + jnp.arange(fresh_count, dtype=jnp.int32), cache_len]
    ).astype(jnp.float32)
    queries = rotate(norm_rows(q_raw, q_gain), places).astype(jnp.bfloat16)
    keys_new = rotate(norm_rows(k_raw, k_gain), places).astype(jnp.bfloat16)
    pre_out = prefill_full(
        queries[:fresh_count],
        key_prefix[0, :, 0:head_dim],
        value_prefix[0, :, 0:head_dim],
        keys_new[:fresh_count, 0],
        v_new[:fresh_count, 0],
        prefill_start[0],
    )
    dec_out = decode_attend(
        queries[fresh_count:],
        key_cache,
        value_cache,
        keys_new[fresh_count:, 0],
        v_new[fresh_count:, 0],
        cache_len,
    )
    pieces = jnp.concatenate([pre_out, dec_out], axis=0)
    pieces, gate_w, up_w, down_w = lax.optimization_barrier((pieces, gate_w, up_w, down_w))
    attended = lax.all_gather(pieces.reshape(tok_req, q_cols), "kv", axis=1, tiled=True)
    resid = (
        rows_all.astype(jnp.float32) + jnp.dot(attended, o_full, preferred_element_type=jnp.float32)
    ).astype(jnp.bfloat16)
    ffn_in = norm_rows(resid, ffn_gain).astype(jnp.bfloat16)
    gate_part = jnp.dot(ffn_in, gate_w, preferred_element_type=jnp.float32)
    up_part = jnp.dot(ffn_in, up_w, preferred_element_type=jnp.float32)
    hidden_act = (jax.nn.silu(gate_part) * up_part).astype(jnp.bfloat16)
    down_part = jnp.dot(hidden_act, down_w, preferred_element_type=jnp.float32)
    tail_count = tok_req - fresh_count + 1
    tail_pad = -(-tail_count // 8) * 8
    scatter_in = jnp.concatenate(
        [
            down_part.reshape(kv_count, rows_dev, model_dim),
            jnp.broadcast_to(down_part[None, tok_req - tail_pad :], (kv_count, tail_pad, model_dim)),
        ],
        axis=1,
    ).reshape(kv_count * (rows_dev + tail_pad), model_dim)
    scattered = lax.psum_scatter(scatter_in, "kv", scatter_dimension=0, tiled=True)
    ffn_part = scattered[:rows_dev]
    tail_sum = scattered[rows_dev + tail_pad - tail_count :]
    mine = lax.dynamic_slice_in_dim(resid, kv_index * rows_dev, rows_dev, axis=0)
    out_rows = (mine.astype(jnp.float32) + ffn_part).astype(jnp.bfloat16)
    going_back = jnp.zeros_like(out_rows).at[slot_place].set(out_rows)
    returned = regroup(going_back)
    layer_out = jnp.zeros_like(hidden_in).at[send_rows].set(returned)
    tail_out = (resid[fresh_count - 1 :].astype(jnp.float32) + tail_sum).astype(jnp.bfloat16)
    tail_rows = norm_rows(tail_out, final_gain).astype(jnp.bfloat16)
    local_peaks = jnp.max(
        jnp.dot(
            lax.all_gather(tail_rows, "req", axis=0, tiled=True),
            lm_head,
            preferred_element_type=jnp.float32,
        ),
        axis=1,
    )
    max_logit = jnp.max(lax.all_gather(local_peaks, ("req", "kv"), axis=0), axis=0)
    return (layer_out, max_logit)


def solution(mesh):
    placed = (
        P(("req", "kv"), None),
        P(),
        P("req"),
        P("req"),
        P("req", None, "kv"),
        P("req", None, "kv"),
        P("req", None, "kv"),
        P("req", None, "kv"),
        P(),
        P(None, "kv"),
        P(None, "kv"),
        P(None, "kv"),
        P(),
        P(),
        P("kv", None),
        P(),
        P(None, "req"),
        P(None, "req"),
        P("req", None),
        P(),
        P(None, ("req", "kv")),
    )
    return jax.shard_map(
        shards, mesh=mesh, in_specs=placed, out_specs=(P(("req", "kv"), None), P()), check_vma=False
    )
```

```python
import jax
import jax.numpy as jnp
from jax import lax
from jax.sharding import PartitionSpec as P

EPS = 1e-06
NEG = -1e30


def spread(value, axis, root):
    mine = lax.axis_index(axis) == root
    return lax.psum(jnp.where(mine, value, jnp.zeros_like(value)), axis)


def norm_rows(values, gain_vec):
    wide = values.astype(jnp.float32)
    return wide * lax.rsqrt(jnp.mean(wide * wide, axis=-1, keepdims=True) + EPS) * gain_vec


def rotate(values, places):
    half_dim = values.shape[-1] // 2
    freqs = 1000000.0 ** (-(jnp.arange(half_dim, dtype=jnp.float32) * 2.0 / values.shape[-1]))
    angles = places[:, None] * freqs[None, :]
    cosine = jnp.cos(angles)[:, None, :]
    sine = jnp.sin(angles)[:, None, :]
    first_half = values[..., :half_dim]
    second_half = values[..., half_dim:]
    return jnp.concatenate(
        [first_half * cosine - second_half * sine, second_half * cosine + first_half * sine],
        axis=-1,
    )


def prefill_full(q_heads, key_old, value_old, key_new, value_new, start_at):
    old_len = key_old.shape[0]
    fresh_rows = q_heads.shape[0]
    factor = q_heads.shape[-1] ** (-0.5)
    all_keys = jnp.concatenate([key_old, key_new], axis=0)
    all_values = jnp.concatenate([value_old, value_new], axis=0)
    scores = (
        jnp.einsum("cgd,kd->gck", q_heads, all_keys, preferred_element_type=jnp.float32) * factor
    )
    key_index = jnp.arange(old_len + fresh_rows, dtype=jnp.int32)[None, :]
    row_index = jnp.arange(fresh_rows, dtype=jnp.int32)[:, None]
    allowed = jnp.where(key_index < old_len, key_index < start_at, key_index - old_len <= row_index)
    scores = jnp.where(allowed[None], scores, NEG)
    row_peak = jnp.max(scores, axis=-1, keepdims=True)
    expd = jnp.exp(scores - row_peak)
    weights = (expd / jnp.sum(expd, axis=-1, keepdims=True)).astype(jnp.bfloat16)
    return jnp.einsum(
        "gck,kd->cgd", weights, all_values, preferred_element_type=jnp.float32
    ).astype(jnp.bfloat16)


def decode_attend(q_heads, key_old, value_old, key_self, value_self, lengths):
    factor = q_heads.shape[-1] ** (-0.5)
    past = jnp.einsum("bgd,bld->bgl", q_heads, key_old, preferred_element_type=jnp.float32) * factor
    slot_index = jnp.arange(key_old.shape[1], dtype=jnp.int32)
    past = jnp.where(slot_index[None, None, :] < lengths[:, None, None], past, NEG)
    own_score = (
        jnp.einsum("bgd,bd->bg", q_heads, key_self, preferred_element_type=jnp.float32) * factor
    )
    row_peak = jnp.maximum(jnp.max(past, axis=-1), own_score)
    past_exp = jnp.exp(past - row_peak[..., None])
    own_exp = jnp.exp(own_score - row_peak)
    row_total = jnp.sum(past_exp, axis=-1) + own_exp
    past_w = (past_exp / row_total[..., None]).astype(jnp.bfloat16)
    own_w = (own_exp / row_total).astype(jnp.bfloat16)
    summed = jnp.einsum("bgl,bld->bgd", past_w, value_old, preferred_element_type=jnp.float32)
    summed = (
        summed + own_w.astype(jnp.float32)[..., None] * value_self.astype(jnp.float32)[:, None, :]
    )
    return summed.astype(jnp.bfloat16)


def regroup(rows_in):
    return lax.all_to_all(rows_in, ("req", "kv"), split_axis=0, concat_axis=0, tiled=True)


def shards(
    hidden_in,
    slot_tokens,
    cache_len,
    prefill_start,
    key_cache,
    value_cache,
    key_prefix,
    value_prefix,
    attn_gain,
    q_proj,
    k_proj,
    v_proj,
    q_gain,
    k_gain,
    o_proj,
    ffn_gain,
    w_gate,
    w_up,
    w_down,
    final_gain,
    lm_head,
):
    req_count = lax.axis_size("req")
    kv_count = lax.axis_size("kv")
    devices = req_count * kv_count
    rows_dev = hidden_in.shape[0]
    kv_index = lax.axis_index("kv")
    self_index = lax.axis_index("req") * kv_count + kv_index
    slot_table = slot_tokens.reshape(devices, rows_dev)
    from_self = slot_table // rows_dev == self_index
    send_rows = jnp.sum(jnp.where(from_self, slot_table - self_index * rows_dev, 0), axis=1)
    slot_place = lax.dynamic_index_in_dim(slot_table, self_index, 0, keepdims=False) // rows_dev
    arrived = regroup(hidden_in[send_rows])
    owner_rows = arrived[slot_place]
    rows_all = lax.all_gather(owner_rows, "kv", axis=0, tiled=True)
    normed = norm_rows(rows_all, attn_gain).astype(jnp.bfloat16)
    o_full = lax.all_to_all(
        jnp.broadcast_to(o_proj[None], (kv_count,) + o_proj.shape), "kv", split_axis=0, concat_axis=0, tiled=True
    ).reshape(kv_count * o_proj.shape[0], o_proj.shape[1])
    ff_dev = w_gate.shape[1]
    ff_piece = ff_dev // kv_count
    weight_piece = jnp.concatenate(
        [
            lax.dynamic_slice_in_dim(w_gate, kv_index * ff_piece, ff_piece, axis=1),
            lax.dynamic_slice_in_dim(w_up, kv_index * ff_piece, ff_piece, axis=1),
            lax.dynamic_slice_in_dim(w_down, kv_index * ff_piece, ff_piece, axis=0).T,
        ],
        axis=1,
    )
    weight_all = lax.all_gather(weight_piece, "req", axis=0)
    model_dim = w_gate.shape[0]
    gate_w = weight_all[:, :, :ff_piece].transpose(1, 0, 2).reshape(model_dim, req_count * ff_piece)
    up_w = weight_all[:, :, ff_piece : 2 * ff_piece].transpose(1, 0, 2).reshape(
        model_dim, req_count * ff_piece
    )
    down_w = weight_all[:, :, 2 * ff_piece :].transpose(0, 2, 1).reshape(req_count * ff_piece, model_dim)
    q_cols = q_proj.shape[1]
    kv_cols = k_proj.shape[1]
    projected = jnp.concatenate(
        [
            jnp.dot(normed, q_proj, preferred_element_type=jnp.float32),
            jnp.dot(normed, k_proj, preferred_element_type=jnp.float32),
            jnp.dot(normed, v_proj, preferred_element_type=jnp.float32),
        ],
        axis=1,
    )
    tok_req = projected.shape[0]
    head_dim = q_gain.shape[0]
    dec_count = cache_len.shape[0]
    fresh_count = tok_req - dec_count
    q_raw = projected[:, :q_cols].reshape(tok_req, q_cols // head_dim, head_dim)
    k_raw = projected[:, q_cols : q_cols + kv_cols].reshape(tok_req, kv_cols // head_dim, head_dim)
    v_new = (
        projected[:, q_cols + kv_cols :]
        .astype(jnp.bfloat16)
        .reshape(tok_req, kv_cols // head_dim, head_dim)
    )
    places = jnp.concatenate(
        [prefill_start[0] + jnp.arange(fresh_count, dtype=jnp.int32), cache_len]
    ).astype(jnp.float32)
    queries = rotate(norm_rows(q_raw, q_gain), places).astype(jnp.bfloat16)
    keys_new = rotate(norm_rows(k_raw, k_gain), places).astype(jnp.bfloat16)
    pre_out = prefill_full(
        queries[:fresh_count],
        key_prefix[0, :, 0:head_dim],
        value_prefix[0, :, 0:head_dim],
        keys_new[:fresh_count, 0],
        v_new[:fresh_count, 0],
        prefill_start[0],
    )
    dec_out = decode_attend(
        queries[fresh_count:],
        key_cache,
        value_cache,
        keys_new[fresh_count:, 0],
        v_new[fresh_count:, 0],
        cache_len,
    )
    pieces = jnp.concatenate([pre_out, dec_out], axis=0)
    pieces, gate_w, up_w, down_w, o_full = lax.optimization_barrier((pieces, gate_w, up_w, down_w, o_full))
    attended = lax.all_gather(pieces.reshape(tok_req, q_cols), "kv", axis=1, tiled=True)
    resid = (
        rows_all.astype(jnp.float32) + jnp.dot(attended, o_full, preferred_element_type=jnp.float32)
    ).astype(jnp.bfloat16)
    ffn_in = norm_rows(resid, ffn_gain).astype(jnp.bfloat16)
    gate_part = jnp.dot(ffn_in, gate_w, preferred_element_type=jnp.float32)
    up_part = jnp.dot(ffn_in, up_w, preferred_element_type=jnp.float32)
    hidden_act = (jax.nn.silu(gate_part) * up_part).astype(jnp.bfloat16)
    down_part = jnp.dot(hidden_act, down_w, preferred_element_type=jnp.float32)
    tail_count = tok_req - fresh_count + 1
    tail_pad = -(-tail_count // 8) * 8
    scatter_in = jnp.concatenate(
        [
            down_part.reshape(kv_count, rows_dev, model_dim),
            jnp.broadcast_to(down_part[None, tok_req - tail_pad :], (kv_count, tail_pad, model_dim)),
        ],
        axis=1,
    ).reshape(kv_count * (rows_dev + tail_pad), model_dim)
    scattered = lax.psum_scatter(scatter_in, "kv", scatter_dimension=0, tiled=True)
    ffn_part = scattered[:rows_dev]
    tail_sum = scattered[rows_dev + tail_pad - tail_count :]
    mine = lax.dynamic_slice_in_dim(resid, kv_index * rows_dev, rows_dev, axis=0)
    out_rows = (mine.astype(jnp.float32) + ffn_part).astype(jnp.bfloat16)
    going_back = jnp.zeros_like(out_rows).at[slot_place].set(out_rows)
    returned = regroup(going_back)
    layer_out = jnp.zeros_like(hidden_in).at[send_rows].set(returned)
    tail_out = (resid[fresh_count - 1 :].astype(jnp.float32) + tail_sum).astype(jnp.bfloat16)
    tail_rows = norm_rows(tail_out, final_gain).astype(jnp.bfloat16)
    local_peaks = jnp.max(
        jnp.dot(
            lax.all_gather(tail_rows, "req", axis=0, tiled=True),
            lm_head,
            preferred_element_type=jnp.float32,
        ),
        axis=1,
    )
    max_logit = lax.pmax(local_peaks, ("req", "kv"))
    return (layer_out, max_logit)


def solution(mesh):
    placed = (
        P(("req", "kv"), None),
        P(),
        P("req"),
        P("req"),
        P("req", None, "kv"),
        P("req", None, "kv"),
        P("req", None, "kv"),
        P("req", None, "kv"),
        P(),
        P(None, "kv"),
        P(None, "kv"),
        P(None, "kv"),
        P(),
        P(),
        P("kv", None),
        P(),
        P(None, "req"),
        P(None, "req"),
        P("req", None),
        P(),
        P(None, ("req", "kv")),
    )
    return jax.shard_map(
        shards, mesh=mesh, in_specs=placed, out_specs=(P(("req", "kv"), None), P()), check_vma=False
    )
```

```python
import jax
import jax.numpy as jnp
from jax import lax
from jax.sharding import PartitionSpec as P

EPS = 1e-06
NEG = -1e30


def spread(value, axis, root):
    mine = lax.axis_index(axis) == root
    return lax.psum(jnp.where(mine, value, jnp.zeros_like(value)), axis)


def norm_rows(values, gain_vec):
    wide = values.astype(jnp.float32)
    return wide * lax.rsqrt(jnp.mean(wide * wide, axis=-1, keepdims=True) + EPS) * gain_vec


def rotate(values, places):
    half_dim = values.shape[-1] // 2
    freqs = 1000000.0 ** (-(jnp.arange(half_dim, dtype=jnp.float32) * 2.0 / values.shape[-1]))
    angles = places[:, None] * freqs[None, :]
    cosine = jnp.cos(angles)[:, None, :]
    sine = jnp.sin(angles)[:, None, :]
    first_half = values[..., :half_dim]
    second_half = values[..., half_dim:]
    return jnp.concatenate(
        [first_half * cosine - second_half * sine, second_half * cosine + first_half * sine],
        axis=-1,
    )


def prefill_full(q_heads, key_old, value_old, key_new, value_new, start_at):
    old_len = key_old.shape[0]
    fresh_rows = q_heads.shape[0]
    factor = q_heads.shape[-1] ** (-0.5)
    all_keys = jnp.concatenate([key_old, key_new], axis=0)
    all_values = jnp.concatenate([value_old, value_new], axis=0)
    scores = (
        jnp.einsum("cgd,kd->gck", q_heads, all_keys, preferred_element_type=jnp.float32) * factor
    )
    key_index = jnp.arange(old_len + fresh_rows, dtype=jnp.int32)[None, :]
    row_index = jnp.arange(fresh_rows, dtype=jnp.int32)[:, None]
    allowed = jnp.where(key_index < old_len, key_index < start_at, key_index - old_len <= row_index)
    scores = jnp.where(allowed[None], scores, NEG)
    row_peak = jnp.max(scores, axis=-1, keepdims=True)
    expd = jnp.exp(scores - row_peak)
    weights = (expd / jnp.sum(expd, axis=-1, keepdims=True)).astype(jnp.bfloat16)
    return jnp.einsum(
        "gck,kd->cgd", weights, all_values, preferred_element_type=jnp.float32
    ).astype(jnp.bfloat16)


def decode_attend(q_heads, key_old, value_old, key_self, value_self, lengths):
    factor = q_heads.shape[-1] ** (-0.5)
    past = jnp.einsum("bgd,bld->bgl", q_heads, key_old, preferred_element_type=jnp.float32) * factor
    slot_index = jnp.arange(key_old.shape[1], dtype=jnp.int32)
    past = jnp.where(slot_index[None, None, :] < lengths[:, None, None], past, NEG)
    own_score = (
        jnp.einsum("bgd,bd->bg", q_heads, key_self, preferred_element_type=jnp.float32) * factor
    )
    row_peak = jnp.maximum(jnp.max(past, axis=-1), own_score)
    past_exp = jnp.exp(past - row_peak[..., None])
    own_exp = jnp.exp(own_score - row_peak)
    row_total = jnp.sum(past_exp, axis=-1) + own_exp
    past_w = (past_exp / row_total[..., None]).astype(jnp.bfloat16)
    own_w = (own_exp / row_total).astype(jnp.bfloat16)
    summed = jnp.einsum("bgl,bld->bgd", past_w, value_old, preferred_element_type=jnp.float32)
    summed = (
        summed + own_w.astype(jnp.float32)[..., None] * value_self.astype(jnp.float32)[:, None, :]
    )
    return summed.astype(jnp.bfloat16)


def regroup(rows_in):
    return lax.all_to_all(rows_in, ("req", "kv"), split_axis=0, concat_axis=0, tiled=True)


def shards(
    hidden_in,
    slot_tokens,
    cache_len,
    prefill_start,
    key_cache,
    value_cache,
    key_prefix,
    value_prefix,
    attn_gain,
    q_proj,
    k_proj,
    v_proj,
    q_gain,
    k_gain,
    o_proj,
    ffn_gain,
    w_gate,
    w_up,
    w_down,
    final_gain,
    lm_head,
):
    req_count = lax.axis_size("req")
    kv_count = lax.axis_size("kv")
    devices = req_count * kv_count
    rows_dev = hidden_in.shape[0]
    kv_index = lax.axis_index("kv")
    self_index = lax.axis_index("req") * kv_count + kv_index
    slot_table = slot_tokens.reshape(devices, rows_dev)
    from_self = slot_table // rows_dev == self_index
    send_rows = jnp.sum(jnp.where(from_self, slot_table - self_index * rows_dev, 0), axis=1)
    slot_place = lax.dynamic_index_in_dim(slot_table, self_index, 0, keepdims=False) // rows_dev
    arrived = regroup(hidden_in[send_rows])
    owner_rows = arrived[slot_place]
    rows_all = lax.all_gather(owner_rows, "kv", axis=0, tiled=True)
    normed = norm_rows(rows_all, attn_gain).astype(jnp.bfloat16)
    o_full = lax.all_to_all(
        jnp.broadcast_to(o_proj[None], (kv_count,) + o_proj.shape), "kv", split_axis=0, concat_axis=0, tiled=True
    ).reshape(kv_count * o_proj.shape[0], o_proj.shape[1])
    ff_dev = w_gate.shape[1]
    ff_piece = ff_dev // kv_count
    weight_piece = jnp.stack(
        [
            lax.dynamic_slice_in_dim(w_gate, kv_index * ff_piece, ff_piece, axis=1).T,
            lax.dynamic_slice_in_dim(w_up, kv_index * ff_piece, ff_piece, axis=1).T,
            lax.dynamic_slice_in_dim(w_down, kv_index * ff_piece, ff_piece, axis=0),
        ]
    )
    weight_all = lax.all_gather(weight_piece, "req", axis=1, tiled=True)
    model_dim = w_gate.shape[0]
    gate_w = weight_all[0]
    up_w = weight_all[1]
    down_w = weight_all[2]
    q_cols = q_proj.shape[1]
    kv_cols = k_proj.shape[1]
    projected = jnp.concatenate(
        [
            jnp.dot(normed, q_proj, preferred_element_type=jnp.float32),
            jnp.dot(normed, k_proj, preferred_element_type=jnp.float32),
            jnp.dot(normed, v_proj, preferred_element_type=jnp.float32),
        ],
        axis=1,
    )
    tok_req = projected.shape[0]
    head_dim = q_gain.shape[0]
    dec_count = cache_len.shape[0]
    fresh_count = tok_req - dec_count
    q_raw = projected[:, :q_cols].reshape(tok_req, q_cols // head_dim, head_dim)
    k_raw = projected[:, q_cols : q_cols + kv_cols].reshape(tok_req, kv_cols // head_dim, head_dim)
    v_new = (
        projected[:, q_cols + kv_cols :]
        .astype(jnp.bfloat16)
        .reshape(tok_req, kv_cols // head_dim, head_dim)
    )
    places = jnp.concatenate(
        [prefill_start[0] + jnp.arange(fresh_count, dtype=jnp.int32), cache_len]
    ).astype(jnp.float32)
    queries = rotate(norm_rows(q_raw, q_gain), places).astype(jnp.bfloat16)
    keys_new = rotate(norm_rows(k_raw, k_gain), places).astype(jnp.bfloat16)
    pre_out = prefill_full(
        queries[:fresh_count],
        key_prefix[0, :, 0:head_dim],
        value_prefix[0, :, 0:head_dim],
        keys_new[:fresh_count, 0],
        v_new[:fresh_count, 0],
        prefill_start[0],
    )
    dec_out = decode_attend(
        queries[fresh_count:],
        key_cache,
        value_cache,
        keys_new[fresh_count:, 0],
        v_new[fresh_count:, 0],
        cache_len,
    )
    pieces = jnp.concatenate([pre_out, dec_out], axis=0)
    pieces, gate_w, up_w, down_w, o_full = lax.optimization_barrier((pieces, gate_w, up_w, down_w, o_full))
    attended = lax.all_gather(pieces.reshape(tok_req, q_cols), "kv", axis=1, tiled=True)
    resid = (
        rows_all.astype(jnp.float32) + jnp.dot(attended, o_full, preferred_element_type=jnp.float32)
    ).astype(jnp.bfloat16)
    ffn_in = norm_rows(resid, ffn_gain).astype(jnp.bfloat16)
    contract_last = (((1,), (1,)), ((), ()))
    gate_part = lax.dot_general(ffn_in, gate_w, contract_last, preferred_element_type=jnp.float32)
    up_part = lax.dot_general(ffn_in, up_w, contract_last, preferred_element_type=jnp.float32)
    hidden_act = (jax.nn.silu(gate_part) * up_part).astype(jnp.bfloat16)
    tail_count = tok_req - fresh_count + 1
    tail_pad = -(-tail_count // 8) * 8
    hidden_width = hidden_act.shape[1]
    scatter_rows = jnp.concatenate(
        [
            hidden_act.reshape(kv_count, rows_dev, hidden_width),
            jnp.broadcast_to(hidden_act[None, tok_req - tail_pad :], (kv_count, tail_pad, hidden_width)),
        ],
        axis=1,
    ).reshape(kv_count * (rows_dev + tail_pad), hidden_width)
    scatter_in = jnp.dot(scatter_rows, down_w, preferred_element_type=jnp.float32)
    scattered = lax.psum_scatter(scatter_in, "kv", scatter_dimension=0, tiled=True)
    ffn_part = scattered[:rows_dev]
    tail_sum = scattered[rows_dev + tail_pad - tail_count :]
    mine = lax.dynamic_slice_in_dim(resid, kv_index * rows_dev, rows_dev, axis=0)
    out_rows = (mine.astype(jnp.float32) + ffn_part).astype(jnp.bfloat16)
    going_back = jnp.zeros_like(out_rows).at[slot_place].set(out_rows)
    returned = regroup(going_back)
    layer_out = jnp.zeros_like(hidden_in).at[send_rows].set(returned)
    tail_out = (resid[fresh_count - 1 :].astype(jnp.float32) + tail_sum).astype(jnp.bfloat16)
    tail_rows = norm_rows(tail_out, final_gain).astype(jnp.bfloat16)
    local_peaks = jnp.max(
        jnp.dot(
            lax.all_gather(tail_rows, "req", axis=0, tiled=True),
            lm_head,
            preferred_element_type=jnp.float32,
        ),
        axis=1,
    )
    max_logit = lax.pmax(lax.pmax(local_peaks, "kv"), "req")
    return (layer_out, max_logit)


def solution(mesh):
    placed = (
        P(("req", "kv"), None),
        P(),
        P("req"),
        P("req"),
        P("req", None, "kv"),
        P("req", None, "kv"),
        P("req", None, "kv"),
        P("req", None, "kv"),
        P(),
        P(None, "kv"),
        P(None, "kv"),
        P(None, "kv"),
        P(),
        P(),
        P("kv", None),
        P(),
        P(None, "req"),
        P(None, "req"),
        P("req", None),
        P(),
        P(None, ("req", "kv")),
    )
    return jax.shard_map(
        shards, mesh=mesh, in_specs=placed, out_specs=(P(("req", "kv"), None), P()), check_vma=False
    )
```

```python
import jax
import jax.numpy as jnp
from jax import lax
from jax.sharding import PartitionSpec as P

EPS = 1e-06
NEG = -1e30


def spread(value, axis, root):
    mine = lax.axis_index(axis) == root
    return lax.psum(jnp.where(mine, value, jnp.zeros_like(value)), axis)


def norm_rows(values, gain_vec):
    wide = values.astype(jnp.float32)
    return wide * lax.rsqrt(jnp.mean(wide * wide, axis=-1, keepdims=True) + EPS) * gain_vec


def rotate(values, places):
    half_dim = values.shape[-1] // 2
    freqs = 1000000.0 ** (-(jnp.arange(half_dim, dtype=jnp.float32) * 2.0 / values.shape[-1]))
    angles = places[:, None] * freqs[None, :]
    cosine = jnp.cos(angles)[:, None, :]
    sine = jnp.sin(angles)[:, None, :]
    first_half = values[..., :half_dim]
    second_half = values[..., half_dim:]
    return jnp.concatenate(
        [first_half * cosine - second_half * sine, second_half * cosine + first_half * sine],
        axis=-1,
    )


def prefill_full(q_heads, key_old, value_old, key_new, value_new, start_at):
    old_len = key_old.shape[0]
    fresh_rows = q_heads.shape[0]
    factor = q_heads.shape[-1] ** (-0.5)
    all_keys = jnp.concatenate([key_old, key_new], axis=0)
    all_values = jnp.concatenate([value_old, value_new], axis=0)
    scores = (
        jnp.einsum("cgd,kd->gck", q_heads, all_keys, preferred_element_type=jnp.float32) * factor
    )
    key_index = jnp.arange(old_len + fresh_rows, dtype=jnp.int32)[None, :]
    row_index = jnp.arange(fresh_rows, dtype=jnp.int32)[:, None]
    allowed = jnp.where(key_index < old_len, key_index < start_at, key_index - old_len <= row_index)
    scores = jnp.where(allowed[None], scores, NEG)
    row_peak = jnp.max(scores, axis=-1, keepdims=True)
    expd = jnp.exp(scores - row_peak)
    weights = (expd / jnp.sum(expd, axis=-1, keepdims=True)).astype(jnp.bfloat16)
    return jnp.einsum(
        "gck,kd->cgd", weights, all_values, preferred_element_type=jnp.float32
    ).astype(jnp.bfloat16)


def decode_attend(q_heads, key_old, value_old, key_self, value_self, lengths):
    factor = q_heads.shape[-1] ** (-0.5)
    past = jnp.einsum("bgd,bld->bgl", q_heads, key_old, preferred_element_type=jnp.float32) * factor
    slot_index = jnp.arange(key_old.shape[1], dtype=jnp.int32)
    past = jnp.where(slot_index[None, None, :] < lengths[:, None, None], past, NEG)
    own_score = (
        jnp.einsum("bgd,bd->bg", q_heads, key_self, preferred_element_type=jnp.float32) * factor
    )
    row_peak = jnp.maximum(jnp.max(past, axis=-1), own_score)
    past_exp = jnp.exp(past - row_peak[..., None])
    own_exp = jnp.exp(own_score - row_peak)
    row_total = jnp.sum(past_exp, axis=-1) + own_exp
    past_w = (past_exp / row_total[..., None]).astype(jnp.bfloat16)
    own_w = (own_exp / row_total).astype(jnp.bfloat16)
    summed = jnp.einsum("bgl,bld->bgd", past_w, value_old, preferred_element_type=jnp.float32)
    summed = (
        summed + own_w.astype(jnp.float32)[..., None] * value_self.astype(jnp.float32)[:, None, :]
    )
    return summed.astype(jnp.bfloat16)


def regroup(rows_in):
    return lax.all_to_all(rows_in, ("req", "kv"), split_axis=0, concat_axis=0, tiled=True)


def shards(
    hidden_in,
    slot_tokens,
    cache_len,
    prefill_start,
    key_cache,
    value_cache,
    key_prefix,
    value_prefix,
    attn_gain,
    q_proj,
    k_proj,
    v_proj,
    q_gain,
    k_gain,
    o_proj,
    ffn_gain,
    w_gate,
    w_up,
    w_down,
    final_gain,
    lm_head,
):
    req_count = lax.axis_size("req")
    kv_count = lax.axis_size("kv")
    devices = req_count * kv_count
    rows_dev = hidden_in.shape[0]
    kv_index = lax.axis_index("kv")
    self_index = lax.axis_index("req") * kv_count + kv_index
    slot_table = slot_tokens.reshape(devices, rows_dev)
    from_self = slot_table // rows_dev == self_index
    send_rows = jnp.sum(jnp.where(from_self, slot_table - self_index * rows_dev, 0), axis=1)
    slot_place = lax.dynamic_index_in_dim(slot_table, self_index, 0, keepdims=False) // rows_dev
    arrived = regroup(hidden_in[send_rows])
    owner_rows = arrived[slot_place]
    rows_all = lax.all_gather(owner_rows, "kv", axis=0, tiled=True)
    normed = norm_rows(rows_all, attn_gain).astype(jnp.bfloat16)
    o_full = lax.all_to_all(
        jnp.broadcast_to(o_proj[None], (kv_count,) + o_proj.shape), "kv", split_axis=0, concat_axis=0, tiled=True
    ).reshape(kv_count * o_proj.shape[0], o_proj.shape[1])
    ff_dev = w_gate.shape[1]
    ff_piece = ff_dev // kv_count
    weight_piece = jnp.stack(
        [
            lax.dynamic_slice_in_dim(w_gate, kv_index * ff_piece, ff_piece, axis=1).T,
            lax.dynamic_slice_in_dim(w_up, kv_index * ff_piece, ff_piece, axis=1).T,
            lax.dynamic_slice_in_dim(w_down, kv_index * ff_piece, ff_piece, axis=0),
        ]
    )
    weight_all = lax.all_gather(weight_piece, "req", axis=1, tiled=True)
    model_dim = w_gate.shape[0]
    gate_w = weight_all[0]
    up_w = weight_all[1]
    down_w = weight_all[2]
    q_cols = q_proj.shape[1]
    kv_cols = k_proj.shape[1]
    projected = jnp.concatenate(
        [
            jnp.dot(normed, q_proj, preferred_element_type=jnp.float32),
            jnp.dot(normed, k_proj, preferred_element_type=jnp.float32),
            jnp.dot(normed, v_proj, preferred_element_type=jnp.float32),
        ],
        axis=1,
    )
    tok_req = projected.shape[0]
    head_dim = q_gain.shape[0]
    dec_count = cache_len.shape[0]
    fresh_count = tok_req - dec_count
    q_raw = projected[:, :q_cols].reshape(tok_req, q_cols // head_dim, head_dim)
    k_raw = projected[:, q_cols : q_cols + kv_cols].reshape(tok_req, kv_cols // head_dim, head_dim)
    v_new = (
        projected[:, q_cols + kv_cols :]
        .astype(jnp.bfloat16)
        .reshape(tok_req, kv_cols // head_dim, head_dim)
    )
    places = jnp.concatenate(
        [prefill_start[0] + jnp.arange(fresh_count, dtype=jnp.int32), cache_len]
    ).astype(jnp.float32)
    queries = rotate(norm_rows(q_raw, q_gain), places).astype(jnp.bfloat16)
    keys_new = rotate(norm_rows(k_raw, k_gain), places).astype(jnp.bfloat16)
    pre_out = prefill_full(
        queries[:fresh_count],
        key_prefix[0, :, 0:head_dim],
        value_prefix[0, :, 0:head_dim],
        keys_new[:fresh_count, 0],
        v_new[:fresh_count, 0],
        prefill_start[0],
    )
    dec_out = decode_attend(
        queries[fresh_count:],
        key_cache,
        value_cache,
        keys_new[fresh_count:, 0],
        v_new[fresh_count:, 0],
        cache_len,
    )
    pieces = jnp.concatenate([pre_out, dec_out], axis=0)
    pieces, gate_w, up_w, down_w, o_full = lax.optimization_barrier((pieces, gate_w, up_w, down_w, o_full))
    attended = lax.all_gather(pieces.reshape(tok_req, q_cols), "kv", axis=1, tiled=True)
    resid = (
        rows_all.astype(jnp.float32) + jnp.dot(attended, o_full, preferred_element_type=jnp.float32)
    ).astype(jnp.bfloat16)
    ffn_in = norm_rows(resid, ffn_gain).astype(jnp.bfloat16)
    contract_last = (((1,), (1,)), ((), ()))
    gate_part = lax.dot_general(ffn_in, gate_w, contract_last, preferred_element_type=jnp.float32)
    up_part = lax.dot_general(ffn_in, up_w, contract_last, preferred_element_type=jnp.float32)
    hidden_act = (jax.nn.silu(gate_part) * up_part).astype(jnp.bfloat16)
    tail_count = tok_req - fresh_count + 1
    tail_pad = -(-tail_count // 8) * 8
    down_part = jnp.dot(hidden_act, down_w, preferred_element_type=jnp.float32)
    ffn_part = lax.psum_scatter(down_part, "kv", scatter_dimension=0, tiled=True)
    tail_part = jnp.dot(hidden_act[tok_req - tail_pad :], down_w, preferred_element_type=jnp.float32)
    tail_parts = lax.all_to_all(
        jnp.broadcast_to(tail_part[None], (kv_count,) + tail_part.shape), "kv", split_axis=0, concat_axis=0, tiled=True
    )
    tail_sum = jnp.sum(tail_parts, axis=0)[tail_pad - tail_count :]
    tail_out = (resid[fresh_count - 1 :].astype(jnp.float32) + tail_sum).astype(jnp.bfloat16)
    tail_rows = norm_rows(tail_out, final_gain).astype(jnp.bfloat16)
    local_peaks = jnp.max(
        jnp.dot(
            lax.all_gather(tail_rows, "req", axis=0, tiled=True),
            lm_head,
            preferred_element_type=jnp.float32,
        ),
        axis=1,
    )
    max_logit = lax.pmax(lax.pmax(local_peaks, "kv"), "req")
    ffn_part, max_logit = lax.optimization_barrier((ffn_part, max_logit))
    mine = lax.dynamic_slice_in_dim(resid, kv_index * rows_dev, rows_dev, axis=0)
    out_rows = (mine.astype(jnp.float32) + ffn_part).astype(jnp.bfloat16)
    going_back = jnp.zeros_like(out_rows).at[slot_place].set(out_rows)
    returned = regroup(going_back)
    layer_out = jnp.zeros_like(hidden_in).at[send_rows].set(returned)
    return (layer_out, max_logit)


def solution(mesh):
    placed = (
        P(("req", "kv"), None),
        P(),
        P("req"),
        P("req"),
        P("req", None, "kv"),
        P("req", None, "kv"),
        P("req", None, "kv"),
        P("req", None, "kv"),
        P(),
        P(None, "kv"),
        P(None, "kv"),
        P(None, "kv"),
        P(),
        P(),
        P("kv", None),
        P(),
        P(None, "req"),
        P(None, "req"),
        P("req", None),
        P(),
        P(None, ("req", "kv")),
    )
    return jax.shard_map(
        shards, mesh=mesh, in_specs=placed, out_specs=(P(("req", "kv"), None), P()), check_vma=False
    )
```

```python
import jax
import jax.numpy as jnp
from jax import lax
from jax.sharding import PartitionSpec as P

EPS = 1e-06
NEG = -1e30


def spread(value, axis, root):
    mine = lax.axis_index(axis) == root
    return lax.psum(jnp.where(mine, value, jnp.zeros_like(value)), axis)


def norm_rows(values, gain_vec):
    wide = values.astype(jnp.float32)
    return wide * lax.rsqrt(jnp.mean(wide * wide, axis=-1, keepdims=True) + EPS) * gain_vec


def rotate(values, places):
    half_dim = values.shape[-1] // 2
    freqs = 1000000.0 ** (-(jnp.arange(half_dim, dtype=jnp.float32) * 2.0 / values.shape[-1]))
    angles = places[:, None] * freqs[None, :]
    cosine = jnp.cos(angles)[:, None, :]
    sine = jnp.sin(angles)[:, None, :]
    first_half = values[..., :half_dim]
    second_half = values[..., half_dim:]
    return jnp.concatenate(
        [first_half * cosine - second_half * sine, second_half * cosine + first_half * sine],
        axis=-1,
    )


def prefill_full(q_heads, key_old, value_old, key_new, value_new, start_at):
    old_len = key_old.shape[0]
    fresh_rows = q_heads.shape[0]
    factor = q_heads.shape[-1] ** (-0.5)
    all_keys = jnp.concatenate([key_old, key_new], axis=0)
    all_values = jnp.concatenate([value_old, value_new], axis=0)
    scores = (
        jnp.einsum("cgd,kd->gck", q_heads, all_keys, preferred_element_type=jnp.float32) * factor
    )
    key_index = jnp.arange(old_len + fresh_rows, dtype=jnp.int32)[None, :]
    row_index = jnp.arange(fresh_rows, dtype=jnp.int32)[:, None]
    allowed = jnp.where(key_index < old_len, key_index < start_at, key_index - old_len <= row_index)
    scores = jnp.where(allowed[None], scores, NEG)
    row_peak = jnp.max(scores, axis=-1, keepdims=True)
    expd = jnp.exp(scores - row_peak)
    weights = (expd / jnp.sum(expd, axis=-1, keepdims=True)).astype(jnp.bfloat16)
    return jnp.einsum(
        "gck,kd->cgd", weights, all_values, preferred_element_type=jnp.float32
    ).astype(jnp.bfloat16)


def decode_attend(q_heads, key_old, value_old, key_self, value_self, lengths):
    factor = q_heads.shape[-1] ** (-0.5)
    past = jnp.einsum("bgd,bld->bgl", q_heads, key_old, preferred_element_type=jnp.float32) * factor
    slot_index = jnp.arange(key_old.shape[1], dtype=jnp.int32)
    past = jnp.where(slot_index[None, None, :] < lengths[:, None, None], past, NEG)
    own_score = (
        jnp.einsum("bgd,bd->bg", q_heads, key_self, preferred_element_type=jnp.float32) * factor
    )
    row_peak = jnp.maximum(jnp.max(past, axis=-1), own_score)
    past_exp = jnp.exp(past - row_peak[..., None])
    own_exp = jnp.exp(own_score - row_peak)
    row_total = jnp.sum(past_exp, axis=-1) + own_exp
    past_w = (past_exp / row_total[..., None]).astype(jnp.bfloat16)
    own_w = (own_exp / row_total).astype(jnp.bfloat16)
    summed = jnp.einsum("bgl,bld->bgd", past_w, value_old, preferred_element_type=jnp.float32)
    summed = (
        summed + own_w.astype(jnp.float32)[..., None] * value_self.astype(jnp.float32)[:, None, :]
    )
    return summed.astype(jnp.bfloat16)


def butterfly(value, axis, combine):
    size = lax.axis_size(axis)
    step = 1
    while step < size:
        pairs = [(i, i ^ step) for i in range(size)]
        value = combine(value, lax.ppermute(value, axis, pairs))
        step *= 2
    return value


def butterfly_gather(value, axis):
    size = lax.axis_size(axis)
    me = lax.axis_index(axis)
    step = 1
    while step < size:
        pairs = [(i, i ^ step) for i in range(size)]
        other = lax.ppermute(value, axis, pairs)
        low = (me // step) % 2 == 0
        value = jnp.concatenate(
            [jnp.where(low, value, other), jnp.where(low, other, value)], axis=0
        )
        step *= 2
    return value


def regroup(rows_in):
    return lax.all_to_all(rows_in, ("req", "kv"), split_axis=0, concat_axis=0, tiled=True)


def shards(
    hidden_in,
    slot_tokens,
    cache_len,
    prefill_start,
    key_cache,
    value_cache,
    key_prefix,
    value_prefix,
    attn_gain,
    q_proj,
    k_proj,
    v_proj,
    q_gain,
    k_gain,
    o_proj,
    ffn_gain,
    w_gate,
    w_up,
    w_down,
    final_gain,
    lm_head,
):
    req_count = lax.axis_size("req")
    kv_count = lax.axis_size("kv")
    devices = req_count * kv_count
    rows_dev = hidden_in.shape[0]
    kv_index = lax.axis_index("kv")
    self_index = lax.axis_index("req") * kv_count + kv_index
    slot_table = slot_tokens.reshape(devices, rows_dev)
    from_self = slot_table // rows_dev == self_index
    send_rows = jnp.sum(jnp.where(from_self, slot_table - self_index * rows_dev, 0), axis=1)
    slot_place = lax.dynamic_index_in_dim(slot_table, self_index, 0, keepdims=False) // rows_dev
    arrived = regroup(hidden_in[send_rows])
    owner_rows = arrived[slot_place]
    rows_all = lax.all_gather(owner_rows, "kv", axis=0, tiled=True)
    normed = norm_rows(rows_all, attn_gain).astype(jnp.bfloat16)
    o_full = lax.all_to_all(
        jnp.broadcast_to(o_proj[None], (kv_count,) + o_proj.shape), "kv", split_axis=0, concat_axis=0, tiled=True
    ).reshape(kv_count * o_proj.shape[0], o_proj.shape[1])
    ff_dev = w_gate.shape[1]
    ff_piece = ff_dev // kv_count
    weight_piece = jnp.stack(
        [
            lax.dynamic_slice_in_dim(w_gate, kv_index * ff_piece, ff_piece, axis=1).T,
            lax.dynamic_slice_in_dim(w_up, kv_index * ff_piece, ff_piece, axis=1).T,
            lax.dynamic_slice_in_dim(w_down, kv_index * ff_piece, ff_piece, axis=0),
        ]
    )
    weight_all = lax.all_gather(weight_piece, "req", axis=1, tiled=True)
    model_dim = w_gate.shape[0]
    gate_w = weight_all[0]
    up_w = weight_all[1]
    down_w = weight_all[2]
    q_cols = q_proj.shape[1]
    kv_cols = k_proj.shape[1]
    projected = jnp.concatenate(
        [
            jnp.dot(normed, q_proj, preferred_element_type=jnp.float32),
            jnp.dot(normed, k_proj, preferred_element_type=jnp.float32),
            jnp.dot(normed, v_proj, preferred_element_type=jnp.float32),
        ],
        axis=1,
    )
    tok_req = projected.shape[0]
    head_dim = q_gain.shape[0]
    dec_count = cache_len.shape[0]
    fresh_count = tok_req - dec_count
    q_raw = projected[:, :q_cols].reshape(tok_req, q_cols // head_dim, head_dim)
    k_raw = projected[:, q_cols : q_cols + kv_cols].reshape(tok_req, kv_cols // head_dim, head_dim)
    v_new = (
        projected[:, q_cols + kv_cols :]
        .astype(jnp.bfloat16)
        .reshape(tok_req, kv_cols // head_dim, head_dim)
    )
    places = jnp.concatenate(
        [prefill_start[0] + jnp.arange(fresh_count, dtype=jnp.int32), cache_len]
    ).astype(jnp.float32)
    queries = rotate(norm_rows(q_raw, q_gain), places).astype(jnp.bfloat16)
    keys_new = rotate(norm_rows(k_raw, k_gain), places).astype(jnp.bfloat16)
    pre_out = prefill_full(
        queries[:fresh_count],
        key_prefix[0, :, 0:head_dim],
        value_prefix[0, :, 0:head_dim],
        keys_new[:fresh_count, 0],
        v_new[:fresh_count, 0],
        prefill_start[0],
    )
    dec_out = decode_attend(
        queries[fresh_count:],
        key_cache,
        value_cache,
        keys_new[fresh_count:, 0],
        v_new[fresh_count:, 0],
        cache_len,
    )
    pieces = jnp.concatenate([pre_out, dec_out], axis=0)
    pieces, gate_w, up_w, down_w, o_full = lax.optimization_barrier((pieces, gate_w, up_w, down_w, o_full))
    attended = lax.all_gather(pieces.reshape(tok_req, q_cols), "kv", axis=1, tiled=True)
    resid = (
        rows_all.astype(jnp.float32) + jnp.dot(attended, o_full, preferred_element_type=jnp.float32)
    ).astype(jnp.bfloat16)
    ffn_in = norm_rows(resid, ffn_gain).astype(jnp.bfloat16)
    contract_last = (((1,), (1,)), ((), ()))
    gate_part = lax.dot_general(ffn_in, gate_w, contract_last, preferred_element_type=jnp.float32)
    up_part = lax.dot_general(ffn_in, up_w, contract_last, preferred_element_type=jnp.float32)
    hidden_act = (jax.nn.silu(gate_part) * up_part).astype(jnp.bfloat16)
    tail_count = tok_req - fresh_count + 1
    tail_pad = -(-tail_count // 8) * 8
    down_part = jnp.dot(hidden_act, down_w, preferred_element_type=jnp.float32)
    ffn_part = lax.psum_scatter(down_part, "kv", scatter_dimension=0, tiled=True)
    tail_part = jnp.dot(hidden_act[tok_req - tail_pad :], down_w, preferred_element_type=jnp.float32)
    tail_sum = butterfly(tail_part, "kv", jnp.add)[tail_pad - tail_count :]
    tail_out = (resid[fresh_count - 1 :].astype(jnp.float32) + tail_sum).astype(jnp.bfloat16)
    tail_rows = norm_rows(tail_out, final_gain).astype(jnp.bfloat16)
    local_peaks = jnp.max(
        jnp.dot(
            butterfly_gather(tail_rows, "req"),
            lm_head,
            preferred_element_type=jnp.float32,
        ),
        axis=1,
    )
    max_logit = butterfly(butterfly(local_peaks, "kv", jnp.maximum), "req", jnp.maximum)
    ffn_part, max_logit = lax.optimization_barrier((ffn_part, max_logit))
    mine = lax.dynamic_slice_in_dim(resid, kv_index * rows_dev, rows_dev, axis=0)
    out_rows = (mine.astype(jnp.float32) + ffn_part).astype(jnp.bfloat16)
    going_back = jnp.zeros_like(out_rows).at[slot_place].set(out_rows)
    returned = regroup(going_back)
    layer_out = jnp.zeros_like(hidden_in).at[send_rows].set(returned)
    return (layer_out, max_logit)


def solution(mesh):
    placed = (
        P(("req", "kv"), None),
        P(),
        P("req"),
        P("req"),
        P("req", None, "kv"),
        P("req", None, "kv"),
        P("req", None, "kv"),
        P("req", None, "kv"),
        P(),
        P(None, "kv"),
        P(None, "kv"),
        P(None, "kv"),
        P(),
        P(),
        P("kv", None),
        P(),
        P(None, "req"),
        P(None, "req"),
        P("req", None),
        P(),
        P(None, ("req", "kv")),
    )
    return jax.shard_map(
        shards, mesh=mesh, in_specs=placed, out_specs=(P(("req", "kv"), None), P()), check_vma=False
    )
```

```python
import jax
import jax.numpy as jnp
from jax import lax
from jax.sharding import PartitionSpec as P

EPS = 1e-06
NEG = -1e30


def spread(value, axis, root):
    mine = lax.axis_index(axis) == root
    return lax.psum(jnp.where(mine, value, jnp.zeros_like(value)), axis)


def norm_rows(values, gain_vec):
    wide = values.astype(jnp.float32)
    return wide * lax.rsqrt(jnp.mean(wide * wide, axis=-1, keepdims=True) + EPS) * gain_vec


def rotate(values, places):
    half_dim = values.shape[-1] // 2
    freqs = 1000000.0 ** (-(jnp.arange(half_dim, dtype=jnp.float32) * 2.0 / values.shape[-1]))
    angles = places[:, None] * freqs[None, :]
    cosine = jnp.cos(angles)[:, None, :]
    sine = jnp.sin(angles)[:, None, :]
    first_half = values[..., :half_dim]
    second_half = values[..., half_dim:]
    return jnp.concatenate(
        [first_half * cosine - second_half * sine, second_half * cosine + first_half * sine],
        axis=-1,
    )


def prefill_full(q_heads, key_old, value_old, key_new, value_new, start_at):
    old_len = key_old.shape[0]
    fresh_rows = q_heads.shape[0]
    factor = q_heads.shape[-1] ** (-0.5)
    all_keys = jnp.concatenate([key_old, key_new], axis=0)
    all_values = jnp.concatenate([value_old, value_new], axis=0)
    scores = (
        jnp.einsum("cgd,kd->gck", q_heads, all_keys, preferred_element_type=jnp.float32) * factor
    )
    key_index = jnp.arange(old_len + fresh_rows, dtype=jnp.int32)[None, :]
    row_index = jnp.arange(fresh_rows, dtype=jnp.int32)[:, None]
    allowed = jnp.where(key_index < old_len, key_index < start_at, key_index - old_len <= row_index)
    scores = jnp.where(allowed[None], scores, NEG)
    row_peak = jnp.max(scores, axis=-1, keepdims=True)
    expd = jnp.exp(scores - row_peak)
    weights = (expd / jnp.sum(expd, axis=-1, keepdims=True)).astype(jnp.bfloat16)
    return jnp.einsum(
        "gck,kd->cgd", weights, all_values, preferred_element_type=jnp.float32
    ).astype(jnp.bfloat16)


def decode_attend(q_heads, key_old, value_old, key_self, value_self, lengths):
    factor = q_heads.shape[-1] ** (-0.5)
    past = jnp.einsum("bgd,bld->bgl", q_heads, key_old, preferred_element_type=jnp.float32) * factor
    slot_index = jnp.arange(key_old.shape[1], dtype=jnp.int32)
    past = jnp.where(slot_index[None, None, :] < lengths[:, None, None], past, NEG)
    own_score = (
        jnp.einsum("bgd,bd->bg", q_heads, key_self, preferred_element_type=jnp.float32) * factor
    )
    row_peak = jnp.maximum(jnp.max(past, axis=-1), own_score)
    past_exp = jnp.exp(past - row_peak[..., None])
    own_exp = jnp.exp(own_score - row_peak)
    row_total = jnp.sum(past_exp, axis=-1) + own_exp
    past_w = (past_exp / row_total[..., None]).astype(jnp.bfloat16)
    own_w = (own_exp / row_total).astype(jnp.bfloat16)
    summed = jnp.einsum("bgl,bld->bgd", past_w, value_old, preferred_element_type=jnp.float32)
    summed = (
        summed + own_w.astype(jnp.float32)[..., None] * value_self.astype(jnp.float32)[:, None, :]
    )
    return summed.astype(jnp.bfloat16)


def direct_reduce(value, axis, combine):
    size = lax.axis_size(axis)
    total = value
    for shift in range(1, size):
        pairs = [(i, (i + shift) % size) for i in range(size)]
        total = combine(total, lax.ppermute(value, axis, pairs))
    return total


def direct_gather(value, axis):
    size = lax.axis_size(axis)
    me = lax.axis_index(axis)
    received = [value]
    for shift in range(1, size):
        pairs = [(i, (i + shift) % size) for i in range(size)]
        received.append(lax.ppermute(value, axis, pairs))
    order = (me - jnp.arange(size, dtype=jnp.int32)) % size
    stacked = jnp.stack(received)[order]
    return stacked.reshape((size * value.shape[0],) + value.shape[1:])


def regroup(rows_in):
    return lax.all_to_all(rows_in, ("req", "kv"), split_axis=0, concat_axis=0, tiled=True)


def shards(
    hidden_in,
    slot_tokens,
    cache_len,
    prefill_start,
    key_cache,
    value_cache,
    key_prefix,
    value_prefix,
    attn_gain,
    q_proj,
    k_proj,
    v_proj,
    q_gain,
    k_gain,
    o_proj,
    ffn_gain,
    w_gate,
    w_up,
    w_down,
    final_gain,
    lm_head,
):
    req_count = lax.axis_size("req")
    kv_count = lax.axis_size("kv")
    devices = req_count * kv_count
    rows_dev = hidden_in.shape[0]
    kv_index = lax.axis_index("kv")
    self_index = lax.axis_index("req") * kv_count + kv_index
    slot_table = slot_tokens.reshape(devices, rows_dev)
    from_self = slot_table // rows_dev == self_index
    send_rows = jnp.sum(jnp.where(from_self, slot_table - self_index * rows_dev, 0), axis=1)
    slot_place = lax.dynamic_index_in_dim(slot_table, self_index, 0, keepdims=False) // rows_dev
    arrived = regroup(hidden_in[send_rows])
    owner_rows = arrived[slot_place]
    rows_all = lax.all_gather(owner_rows, "kv", axis=0, tiled=True)
    normed = norm_rows(rows_all, attn_gain).astype(jnp.bfloat16)
    o_full = lax.all_to_all(
        jnp.broadcast_to(o_proj[None], (kv_count,) + o_proj.shape), "kv", split_axis=0, concat_axis=0, tiled=True
    ).reshape(kv_count * o_proj.shape[0], o_proj.shape[1])
    ff_dev = w_gate.shape[1]
    ff_piece = ff_dev // kv_count
    weight_piece = jnp.stack(
        [
            lax.dynamic_slice_in_dim(w_gate, kv_index * ff_piece, ff_piece, axis=1).T,
            lax.dynamic_slice_in_dim(w_up, kv_index * ff_piece, ff_piece, axis=1).T,
            lax.dynamic_slice_in_dim(w_down, kv_index * ff_piece, ff_piece, axis=0),
        ]
    )
    weight_all = lax.all_gather(weight_piece, "req", axis=1, tiled=True)
    model_dim = w_gate.shape[0]
    gate_w = weight_all[0]
    up_w = weight_all[1]
    down_w = weight_all[2]
    q_cols = q_proj.shape[1]
    kv_cols = k_proj.shape[1]
    projected = jnp.concatenate(
        [
            jnp.dot(normed, q_proj, preferred_element_type=jnp.float32),
            jnp.dot(normed, k_proj, preferred_element_type=jnp.float32),
            jnp.dot(normed, v_proj, preferred_element_type=jnp.float32),
        ],
        axis=1,
    )
    tok_req = projected.shape[0]
    head_dim = q_gain.shape[0]
    dec_count = cache_len.shape[0]
    fresh_count = tok_req - dec_count
    q_raw = projected[:, :q_cols].reshape(tok_req, q_cols // head_dim, head_dim)
    k_raw = projected[:, q_cols : q_cols + kv_cols].reshape(tok_req, kv_cols // head_dim, head_dim)
    v_new = (
        projected[:, q_cols + kv_cols :]
        .astype(jnp.bfloat16)
        .reshape(tok_req, kv_cols // head_dim, head_dim)
    )
    places = jnp.concatenate(
        [prefill_start[0] + jnp.arange(fresh_count, dtype=jnp.int32), cache_len]
    ).astype(jnp.float32)
    queries = rotate(norm_rows(q_raw, q_gain), places).astype(jnp.bfloat16)
    keys_new = rotate(norm_rows(k_raw, k_gain), places).astype(jnp.bfloat16)
    pre_out = prefill_full(
        queries[:fresh_count],
        key_prefix[0, :, 0:head_dim],
        value_prefix[0, :, 0:head_dim],
        keys_new[:fresh_count, 0],
        v_new[:fresh_count, 0],
        prefill_start[0],
    )
    dec_out = decode_attend(
        queries[fresh_count:],
        key_cache,
        value_cache,
        keys_new[fresh_count:, 0],
        v_new[fresh_count:, 0],
        cache_len,
    )
    pieces = jnp.concatenate([pre_out, dec_out], axis=0)
    pieces, gate_w, up_w, down_w, o_full = lax.optimization_barrier((pieces, gate_w, up_w, down_w, o_full))
    attended = lax.all_gather(pieces.reshape(tok_req, q_cols), "kv", axis=1, tiled=True)
    resid = (
        rows_all.astype(jnp.float32) + jnp.dot(attended, o_full, preferred_element_type=jnp.float32)
    ).astype(jnp.bfloat16)
    ffn_in = norm_rows(resid, ffn_gain).astype(jnp.bfloat16)
    contract_last = (((1,), (1,)), ((), ()))
    gate_part = lax.dot_general(ffn_in, gate_w, contract_last, preferred_element_type=jnp.float32)
    up_part = lax.dot_general(ffn_in, up_w, contract_last, preferred_element_type=jnp.float32)
    hidden_act = (jax.nn.silu(gate_part) * up_part).astype(jnp.bfloat16)
    tail_count = tok_req - fresh_count + 1
    tail_pad = -(-tail_count // 8) * 8
    down_part = jnp.dot(hidden_act, down_w, preferred_element_type=jnp.float32)
    ffn_part = lax.psum_scatter(down_part, "kv", scatter_dimension=0, tiled=True)
    tail_part = jnp.dot(hidden_act[tok_req - tail_pad :], down_w, preferred_element_type=jnp.float32)
    tail_sum = direct_reduce(tail_part, "kv", jnp.add)[tail_pad - tail_count :]
    tail_out = (resid[fresh_count - 1 :].astype(jnp.float32) + tail_sum).astype(jnp.bfloat16)
    tail_rows = norm_rows(tail_out, final_gain).astype(jnp.bfloat16)
    local_peaks = jnp.max(
        jnp.dot(
            direct_gather(tail_rows, "req"),
            lm_head,
            preferred_element_type=jnp.float32,
        ),
        axis=1,
    )
    max_logit = direct_reduce(direct_reduce(local_peaks, "kv", jnp.maximum), "req", jnp.maximum)
    ffn_part, max_logit = lax.optimization_barrier((ffn_part, max_logit))
    mine = lax.dynamic_slice_in_dim(resid, kv_index * rows_dev, rows_dev, axis=0)
    out_rows = (mine.astype(jnp.float32) + ffn_part).astype(jnp.bfloat16)
    going_back = jnp.zeros_like(out_rows).at[slot_place].set(out_rows)
    returned = regroup(going_back)
    layer_out = jnp.zeros_like(hidden_in).at[send_rows].set(returned)
    return (layer_out, max_logit)


def solution(mesh):
    placed = (
        P(("req", "kv"), None),
        P(),
        P("req"),
        P("req"),
        P("req", None, "kv"),
        P("req", None, "kv"),
        P("req", None, "kv"),
        P("req", None, "kv"),
        P(),
        P(None, "kv"),
        P(None, "kv"),
        P(None, "kv"),
        P(),
        P(),
        P("kv", None),
        P(),
        P(None, "req"),
        P(None, "req"),
        P("req", None),
        P(),
        P(None, ("req", "kv")),
    )
    return jax.shard_map(
        shards, mesh=mesh, in_specs=placed, out_specs=(P(("req", "kv"), None), P()), check_vma=False
    )
```

```python
import jax
import jax.numpy as jnp
from jax import lax
from jax.sharding import PartitionSpec as P

EPS = 1e-06
NEG = -1e30


def spread(value, axis, root):
    mine = lax.axis_index(axis) == root
    return lax.psum(jnp.where(mine, value, jnp.zeros_like(value)), axis)


def norm_rows(values, gain_vec):
    wide = values.astype(jnp.float32)
    return wide * lax.rsqrt(jnp.mean(wide * wide, axis=-1, keepdims=True) + EPS) * gain_vec


def rotate(values, places):
    half_dim = values.shape[-1] // 2
    freqs = 1000000.0 ** (-(jnp.arange(half_dim, dtype=jnp.float32) * 2.0 / values.shape[-1]))
    angles = places[:, None] * freqs[None, :]
    cosine = jnp.cos(angles)[:, None, :]
    sine = jnp.sin(angles)[:, None, :]
    first_half = values[..., :half_dim]
    second_half = values[..., half_dim:]
    return jnp.concatenate(
        [first_half * cosine - second_half * sine, second_half * cosine + first_half * sine],
        axis=-1,
    )


def prefill_full(q_heads, key_old, value_old, key_new, value_new, start_at):
    old_len = key_old.shape[0]
    fresh_rows = q_heads.shape[0]
    factor = q_heads.shape[-1] ** (-0.5)
    all_keys = jnp.concatenate([key_old, key_new], axis=0)
    all_values = jnp.concatenate([value_old, value_new], axis=0)
    scores = (
        jnp.einsum("cgd,kd->gck", q_heads, all_keys, preferred_element_type=jnp.float32) * factor
    )
    key_index = jnp.arange(old_len + fresh_rows, dtype=jnp.int32)[None, :]
    row_index = jnp.arange(fresh_rows, dtype=jnp.int32)[:, None]
    allowed = jnp.where(key_index < old_len, key_index < start_at, key_index - old_len <= row_index)
    scores = jnp.where(allowed[None], scores, NEG)
    row_peak = jnp.max(scores, axis=-1, keepdims=True)
    expd = jnp.exp(scores - row_peak)
    weights = (expd / jnp.sum(expd, axis=-1, keepdims=True)).astype(jnp.bfloat16)
    return jnp.einsum(
        "gck,kd->cgd", weights, all_values, preferred_element_type=jnp.float32
    ).astype(jnp.bfloat16)


def decode_attend(q_heads, key_old, value_old, key_self, value_self, lengths):
    factor = q_heads.shape[-1] ** (-0.5)
    past = jnp.einsum("bgd,bld->bgl", q_heads, key_old, preferred_element_type=jnp.float32) * factor
    slot_index = jnp.arange(key_old.shape[1], dtype=jnp.int32)
    past = jnp.where(slot_index[None, None, :] < lengths[:, None, None], past, NEG)
    own_score = (
        jnp.einsum("bgd,bd->bg", q_heads, key_self, preferred_element_type=jnp.float32) * factor
    )
    row_peak = jnp.maximum(jnp.max(past, axis=-1), own_score)
    past_exp = jnp.exp(past - row_peak[..., None])
    own_exp = jnp.exp(own_score - row_peak)
    row_total = jnp.sum(past_exp, axis=-1) + own_exp
    past_w = (past_exp / row_total[..., None]).astype(jnp.bfloat16)
    own_w = (own_exp / row_total).astype(jnp.bfloat16)
    summed = jnp.einsum("bgl,bld->bgd", past_w, value_old, preferred_element_type=jnp.float32)
    summed = (
        summed + own_w.astype(jnp.float32)[..., None] * value_self.astype(jnp.float32)[:, None, :]
    )
    return summed.astype(jnp.bfloat16)


def butterfly(value, axis, combine):
    size = lax.axis_size(axis)
    step = 1
    while step < size:
        pairs = [(i, i ^ step) for i in range(size)]
        value = combine(value, lax.ppermute(value, axis, pairs))
        step *= 2
    return value


def butterfly_gather(value, axis):
    size = lax.axis_size(axis)
    me = lax.axis_index(axis)
    step = 1
    while step < size:
        pairs = [(i, i ^ step) for i in range(size)]
        other = lax.ppermute(value, axis, pairs)
        low = (me // step) % 2 == 0
        value = jnp.concatenate(
            [jnp.where(low, value, other), jnp.where(low, other, value)], axis=0
        )
        step *= 2
    return value


def regroup(rows_in):
    return lax.all_to_all(rows_in, ("req", "kv"), split_axis=0, concat_axis=0, tiled=True)


def shards(
    hidden_in,
    slot_tokens,
    cache_len,
    prefill_start,
    key_cache,
    value_cache,
    key_prefix,
    value_prefix,
    attn_gain,
    q_proj,
    k_proj,
    v_proj,
    q_gain,
    k_gain,
    o_proj,
    ffn_gain,
    w_gate,
    w_up,
    w_down,
    final_gain,
    lm_head,
):
    req_count = lax.axis_size("req")
    kv_count = lax.axis_size("kv")
    devices = req_count * kv_count
    rows_dev = hidden_in.shape[0]
    kv_index = lax.axis_index("kv")
    self_index = lax.axis_index("req") * kv_count + kv_index
    slot_table = slot_tokens.reshape(devices, rows_dev)
    from_self = slot_table // rows_dev == self_index
    send_rows = jnp.sum(jnp.where(from_self, slot_table - self_index * rows_dev, 0), axis=1)
    slot_place = lax.dynamic_index_in_dim(slot_table, self_index, 0, keepdims=False) // rows_dev
    arrived = regroup(hidden_in[send_rows])
    owner_rows = arrived[slot_place]
    rows_all = lax.all_gather(owner_rows, "kv", axis=0, tiled=True)
    normed = norm_rows(rows_all, attn_gain).astype(jnp.bfloat16)
    o_local, rows_all = lax.optimization_barrier((o_proj, rows_all))
    o_full = lax.all_to_all(
        jnp.broadcast_to(o_local[None], (kv_count,) + o_proj.shape), "kv", split_axis=0, concat_axis=0, tiled=True
    ).reshape(kv_count * o_local.shape[0], o_local.shape[1])
    ff_dev = w_gate.shape[1]
    ff_piece = ff_dev // kv_count
    weight_piece = jnp.stack(
        [
            lax.dynamic_slice_in_dim(w_gate, kv_index * ff_piece, ff_piece, axis=1).T,
            lax.dynamic_slice_in_dim(w_up, kv_index * ff_piece, ff_piece, axis=1).T,
            lax.dynamic_slice_in_dim(w_down, kv_index * ff_piece, ff_piece, axis=0),
        ]
    )
    weight_all = lax.all_gather(weight_piece, "req", axis=1, tiled=True)
    model_dim = w_gate.shape[0]
    q_cols = q_proj.shape[1]
    kv_cols = k_proj.shape[1]
    projected = jnp.concatenate(
        [
            jnp.dot(normed, q_proj, preferred_element_type=jnp.float32),
            jnp.dot(normed, k_proj, preferred_element_type=jnp.float32),
            jnp.dot(normed, v_proj, preferred_element_type=jnp.float32),
        ],
        axis=1,
    )
    tok_req = projected.shape[0]
    head_dim = q_gain.shape[0]
    dec_count = cache_len.shape[0]
    fresh_count = tok_req - dec_count
    q_raw = projected[:, :q_cols].reshape(tok_req, q_cols // head_dim, head_dim)
    k_raw = projected[:, q_cols : q_cols + kv_cols].reshape(tok_req, kv_cols // head_dim, head_dim)
    v_new = (
        projected[:, q_cols + kv_cols :]
        .astype(jnp.bfloat16)
        .reshape(tok_req, kv_cols // head_dim, head_dim)
    )
    places = jnp.concatenate(
        [prefill_start[0] + jnp.arange(fresh_count, dtype=jnp.int32), cache_len]
    ).astype(jnp.float32)
    queries = rotate(norm_rows(q_raw, q_gain), places).astype(jnp.bfloat16)
    keys_new = rotate(norm_rows(k_raw, k_gain), places).astype(jnp.bfloat16)
    pre_out = prefill_full(
        queries[:fresh_count],
        key_prefix[0, :, 0:head_dim],
        value_prefix[0, :, 0:head_dim],
        keys_new[:fresh_count, 0],
        v_new[:fresh_count, 0],
        prefill_start[0],
    )
    dec_out = decode_attend(
        queries[fresh_count:],
        key_cache,
        value_cache,
        keys_new[fresh_count:, 0],
        v_new[fresh_count:, 0],
        cache_len,
    )
    pieces = jnp.concatenate([pre_out, dec_out], axis=0)
    pieces, weight_all, o_full = lax.optimization_barrier((pieces, weight_all, o_full))
    gate_w = weight_all[0]
    up_w = weight_all[1]
    down_w = weight_all[2]
    attended = lax.all_gather(pieces.reshape(tok_req, q_cols), "kv", axis=1, tiled=True)
    resid = (
        rows_all.astype(jnp.float32) + jnp.dot(attended, o_full, preferred_element_type=jnp.float32)
    ).astype(jnp.bfloat16)
    ffn_in = norm_rows(resid, ffn_gain).astype(jnp.bfloat16)
    contract_last = (((1,), (1,)), ((), ()))
    gate_part = lax.dot_general(ffn_in, gate_w, contract_last, preferred_element_type=jnp.float32)
    up_part = lax.dot_general(ffn_in, up_w, contract_last, preferred_element_type=jnp.float32)
    hidden_act = (jax.nn.silu(gate_part) * up_part).astype(jnp.bfloat16)
    tail_count = tok_req - fresh_count + 1
    tail_pad = -(-tail_count // 8) * 8
    down_part = jnp.dot(hidden_act, down_w, preferred_element_type=jnp.float32)
    ffn_part = lax.psum_scatter(down_part, "kv", scatter_dimension=0, tiled=True)
    tail_part = jnp.dot(hidden_act[tok_req - tail_pad :], down_w, preferred_element_type=jnp.float32)
    tail_sum = butterfly(tail_part, "kv", jnp.add)[tail_pad - tail_count :]
    tail_out = (resid[fresh_count - 1 :].astype(jnp.float32) + tail_sum).astype(jnp.bfloat16)
    tail_rows = norm_rows(tail_out, final_gain).astype(jnp.bfloat16)
    local_peaks = jnp.max(
        jnp.dot(
            butterfly_gather(tail_rows, "req"),
            lm_head,
            preferred_element_type=jnp.float32,
        ),
        axis=1,
    )
    max_logit = butterfly(butterfly(local_peaks, "kv", jnp.maximum), "req", jnp.maximum)
    ffn_part, max_logit = lax.optimization_barrier((ffn_part, max_logit))
    mine = lax.dynamic_slice_in_dim(resid, kv_index * rows_dev, rows_dev, axis=0)
    out_rows = (mine.astype(jnp.float32) + ffn_part).astype(jnp.bfloat16)
    going_back = jnp.zeros_like(out_rows).at[slot_place].set(out_rows)
    returned = regroup(going_back)
    layer_out = jnp.zeros_like(hidden_in).at[send_rows].set(returned)
    return (layer_out, max_logit)


def solution(mesh):
    placed = (
        P(("req", "kv"), None),
        P(),
        P("req"),
        P("req"),
        P("req", None, "kv"),
        P("req", None, "kv"),
        P("req", None, "kv"),
        P("req", None, "kv"),
        P(),
        P(None, "kv"),
        P(None, "kv"),
        P(None, "kv"),
        P(),
        P(),
        P("kv", None),
        P(),
        P(None, "req"),
        P(None, "req"),
        P("req", None),
        P(),
        P(None, ("req", "kv")),
    )
    return jax.shard_map(
        shards, mesh=mesh, in_specs=placed, out_specs=(P(("req", "kv"), None), P()), check_vma=False
    )
```

```python
import jax
import jax.numpy as jnp
from jax import lax
from jax.sharding import PartitionSpec as P

EPS = 1e-06
NEG = -1e30


def spread(value, axis, root):
    mine = lax.axis_index(axis) == root
    return lax.psum(jnp.where(mine, value, jnp.zeros_like(value)), axis)


def norm_rows(values, gain_vec):
    wide = values.astype(jnp.float32)
    return wide * lax.rsqrt(jnp.mean(wide * wide, axis=-1, keepdims=True) + EPS) * gain_vec


def rotate(values, places):
    half_dim = values.shape[-1] // 2
    freqs = 1000000.0 ** (-(jnp.arange(half_dim, dtype=jnp.float32) * 2.0 / values.shape[-1]))
    angles = places[:, None] * freqs[None, :]
    cosine = jnp.cos(angles)[:, None, :]
    sine = jnp.sin(angles)[:, None, :]
    first_half = values[..., :half_dim]
    second_half = values[..., half_dim:]
    return jnp.concatenate(
        [first_half * cosine - second_half * sine, second_half * cosine + first_half * sine],
        axis=-1,
    )


def prefill_full(q_heads, key_old, value_old, key_new, value_new, start_at):
    old_len = key_old.shape[0]
    fresh_rows = q_heads.shape[0]
    factor = q_heads.shape[-1] ** (-0.5)
    all_keys = jnp.concatenate([key_old, key_new], axis=0)
    all_values = jnp.concatenate([value_old, value_new], axis=0)
    scores = (
        jnp.einsum("cgd,kd->gck", q_heads, all_keys, preferred_element_type=jnp.float32) * factor
    )
    key_index = jnp.arange(old_len + fresh_rows, dtype=jnp.int32)[None, :]
    row_index = jnp.arange(fresh_rows, dtype=jnp.int32)[:, None]
    allowed = jnp.where(key_index < old_len, key_index < start_at, key_index - old_len <= row_index)
    scores = jnp.where(allowed[None], scores, NEG)
    row_peak = jnp.max(scores, axis=-1, keepdims=True)
    expd = jnp.exp(scores - row_peak)
    weights = (expd / jnp.sum(expd, axis=-1, keepdims=True)).astype(jnp.bfloat16)
    return jnp.einsum(
        "gck,kd->cgd", weights, all_values, preferred_element_type=jnp.float32
    ).astype(jnp.bfloat16)


def decode_attend(q_heads, key_old, value_old, key_self, value_self, lengths):
    factor = q_heads.shape[-1] ** (-0.5)
    past = jnp.einsum("bgd,bld->bgl", q_heads, key_old, preferred_element_type=jnp.float32) * factor
    slot_index = jnp.arange(key_old.shape[1], dtype=jnp.int32)
    past = jnp.where(slot_index[None, None, :] < lengths[:, None, None], past, NEG)
    own_score = (
        jnp.einsum("bgd,bd->bg", q_heads, key_self, preferred_element_type=jnp.float32) * factor
    )
    row_peak = jnp.maximum(jnp.max(past, axis=-1), own_score)
    past_exp = jnp.exp(past - row_peak[..., None])
    own_exp = jnp.exp(own_score - row_peak)
    row_total = jnp.sum(past_exp, axis=-1) + own_exp
    past_w = (past_exp / row_total[..., None]).astype(jnp.bfloat16)
    own_w = (own_exp / row_total).astype(jnp.bfloat16)
    summed = jnp.einsum("bgl,bld->bgd", past_w, value_old, preferred_element_type=jnp.float32)
    summed = (
        summed + own_w.astype(jnp.float32)[..., None] * value_self.astype(jnp.float32)[:, None, :]
    )
    return summed.astype(jnp.bfloat16)


def butterfly(value, axis, combine):
    size = lax.axis_size(axis)
    step = 1
    while step < size:
        pairs = [(i, i ^ step) for i in range(size)]
        value = combine(value, lax.ppermute(value, axis, pairs))
        step *= 2
    return value


def butterfly_gather(value, axis):
    size = lax.axis_size(axis)
    me = lax.axis_index(axis)
    step = 1
    while step < size:
        pairs = [(i, i ^ step) for i in range(size)]
        other = lax.ppermute(value, axis, pairs)
        low = (me // step) % 2 == 0
        value = jnp.concatenate(
            [jnp.where(low, value, other), jnp.where(low, other, value)], axis=0
        )
        step *= 2
    return value


def regroup(rows_in):
    return lax.all_to_all(rows_in, ("req", "kv"), split_axis=0, concat_axis=0, tiled=True)


def shards(
    hidden_in,
    slot_tokens,
    cache_len,
    prefill_start,
    key_cache,
    value_cache,
    key_prefix,
    value_prefix,
    attn_gain,
    q_proj,
    k_proj,
    v_proj,
    q_gain,
    k_gain,
    o_proj,
    ffn_gain,
    w_gate,
    w_up,
    w_down,
    final_gain,
    lm_head,
):
    req_count = lax.axis_size("req")
    kv_count = lax.axis_size("kv")
    devices = req_count * kv_count
    rows_dev = hidden_in.shape[0]
    kv_index = lax.axis_index("kv")
    self_index = lax.axis_index("req") * kv_count + kv_index
    slot_table = slot_tokens.reshape(devices, rows_dev)
    from_self = slot_table // rows_dev == self_index
    send_rows = jnp.sum(jnp.where(from_self, slot_table - self_index * rows_dev, 0), axis=1)
    slot_place = lax.dynamic_index_in_dim(slot_table, self_index, 0, keepdims=False) // rows_dev
    arrived = regroup(hidden_in[send_rows])
    owner_rows = arrived[slot_place]
    rows_all = lax.all_gather(owner_rows, "kv", axis=0, tiled=True)
    normed = norm_rows(rows_all, attn_gain).astype(jnp.bfloat16)
    o_full = lax.all_to_all(
        jnp.broadcast_to(o_proj[None], (kv_count,) + o_proj.shape), "kv", split_axis=0, concat_axis=0, tiled=True
    ).reshape(kv_count * o_proj.shape[0], o_proj.shape[1])
    ff_dev = w_gate.shape[1]
    ff_piece = ff_dev // kv_count
    weight_piece = jnp.stack(
        [
            lax.dynamic_slice_in_dim(w_gate, kv_index * ff_piece, ff_piece, axis=1).T,
            lax.dynamic_slice_in_dim(w_up, kv_index * ff_piece, ff_piece, axis=1).T,
            lax.dynamic_slice_in_dim(w_down, kv_index * ff_piece, ff_piece, axis=0),
        ]
    )
    weight_all = lax.all_gather(weight_piece, "req", axis=1, tiled=True)
    model_dim = w_gate.shape[0]
    q_cols = q_proj.shape[1]
    kv_cols = k_proj.shape[1]
    projected = jnp.concatenate(
        [
            jnp.dot(normed, q_proj, preferred_element_type=jnp.float32),
            jnp.dot(normed, k_proj, preferred_element_type=jnp.float32),
            jnp.dot(normed, v_proj, preferred_element_type=jnp.float32),
        ],
        axis=1,
    )
    tok_req = projected.shape[0]
    head_dim = q_gain.shape[0]
    dec_count = cache_len.shape[0]
    fresh_count = tok_req - dec_count
    q_raw = projected[:, :q_cols].reshape(tok_req, q_cols // head_dim, head_dim)
    k_raw = projected[:, q_cols : q_cols + kv_cols].reshape(tok_req, kv_cols // head_dim, head_dim)
    v_new = (
        projected[:, q_cols + kv_cols :]
        .astype(jnp.bfloat16)
        .reshape(tok_req, kv_cols // head_dim, head_dim)
    )
    places = jnp.concatenate(
        [prefill_start[0] + jnp.arange(fresh_count, dtype=jnp.int32), cache_len]
    ).astype(jnp.float32)
    queries = rotate(norm_rows(q_raw, q_gain), places).astype(jnp.bfloat16)
    keys_new = rotate(norm_rows(k_raw, k_gain), places).astype(jnp.bfloat16)
    pre_out = prefill_full(
        queries[:fresh_count],
        key_prefix[0, :, 0:head_dim],
        value_prefix[0, :, 0:head_dim],
        keys_new[:fresh_count, 0],
        v_new[:fresh_count, 0],
        prefill_start[0],
    )
    dec_out = decode_attend(
        queries[fresh_count:],
        key_cache,
        value_cache,
        keys_new[fresh_count:, 0],
        v_new[fresh_count:, 0],
        cache_len,
    )
    pieces = jnp.concatenate([pre_out, dec_out], axis=0)
    pieces, weight_all, o_full = lax.optimization_barrier((pieces, weight_all, o_full))
    gate_w = weight_all[0]
    up_w = weight_all[1]
    down_w = weight_all[2]
    attended = lax.all_gather(pieces.reshape(tok_req, q_cols), "kv", axis=1, tiled=True)
    resid = (
        rows_all.astype(jnp.float32) + jnp.dot(attended, o_full, preferred_element_type=jnp.float32)
    ).astype(jnp.bfloat16)
    ffn_in = norm_rows(resid, ffn_gain).astype(jnp.bfloat16)
    contract_last = (((1,), (1,)), ((), ()))
    gate_part = lax.dot_general(ffn_in, gate_w, contract_last, preferred_element_type=jnp.float32)
    up_part = lax.dot_general(ffn_in, up_w, contract_last, preferred_element_type=jnp.float32)
    hidden_act = (jax.nn.silu(gate_part) * up_part).astype(jnp.bfloat16)
    tail_count = tok_req - fresh_count + 1
    tail_pad = -(-tail_count // 8) * 8
    down_part = jnp.dot(hidden_act, down_w, preferred_element_type=jnp.float32)
    ffn_part = lax.psum_scatter(down_part, "kv", scatter_dimension=0, tiled=True)
    tail_part = jnp.dot(hidden_act[tok_req - tail_pad :], down_w, preferred_element_type=jnp.float32)
    tail_sum = butterfly(tail_part, "kv", jnp.add)[tail_pad - tail_count :]
    tail_out = (resid[fresh_count - 1 :].astype(jnp.float32) + tail_sum).astype(jnp.bfloat16)
    tail_rows = norm_rows(tail_out, final_gain).astype(jnp.bfloat16)
    local_peaks = jnp.max(
        jnp.dot(
            butterfly_gather(tail_rows, "req"),
            lm_head,
            preferred_element_type=jnp.float32,
        ),
        axis=1,
    )
    max_logit = butterfly(butterfly(local_peaks, "kv", jnp.maximum), "req", jnp.maximum)
    ffn_part, max_logit = lax.optimization_barrier((ffn_part, max_logit))
    mine = lax.dynamic_slice_in_dim(resid, kv_index * rows_dev, rows_dev, axis=0)
    out_rows = (mine.astype(jnp.float32) + ffn_part).astype(jnp.bfloat16)
    going_back = jnp.zeros_like(out_rows).at[slot_place].set(out_rows)
    returned = regroup(going_back)
    layer_out = jnp.zeros_like(hidden_in).at[send_rows].set(returned)
    return (layer_out, max_logit)


def solution(mesh):
    placed = (
        P(("req", "kv"), None),
        P(),
        P("req"),
        P("req"),
        P("req", None, "kv"),
        P("req", None, "kv"),
        P("req", None, "kv"),
        P("req", None, "kv"),
        P(),
        P(None, "kv"),
        P(None, "kv"),
        P(None, "kv"),
        P(),
        P(),
        P("kv", None),
        P(),
        P(None, "req"),
        P(None, "req"),
        P("req", None),
        P(),
        P(None, ("req", "kv")),
    )
    return jax.shard_map(
        shards, mesh=mesh, in_specs=placed, out_specs=(P(("req", "kv"), None), P()), check_vma=False
    )
```

```python
import jax
import jax.numpy as jnp
from jax import lax
from jax.sharding import PartitionSpec as P

EPS = 1e-06
NEG = -1e30


def spread(value, axis, root):
    mine = lax.axis_index(axis) == root
    return lax.psum(jnp.where(mine, value, jnp.zeros_like(value)), axis)


def norm_rows(values, gain_vec):
    wide = values.astype(jnp.float32)
    return wide * lax.rsqrt(jnp.mean(wide * wide, axis=-1, keepdims=True) + EPS) * gain_vec


def rotate(values, places):
    half_dim = values.shape[-1] // 2
    freqs = 1000000.0 ** (-(jnp.arange(half_dim, dtype=jnp.float32) * 2.0 / values.shape[-1]))
    angles = places[:, None] * freqs[None, :]
    cosine = jnp.cos(angles)[:, None, :]
    sine = jnp.sin(angles)[:, None, :]
    first_half = values[..., :half_dim]
    second_half = values[..., half_dim:]
    return jnp.concatenate(
        [first_half * cosine - second_half * sine, second_half * cosine + first_half * sine],
        axis=-1,
    )


def prefill_full(q_heads, key_old, value_old, key_new, value_new, start_at):
    old_len = key_old.shape[0]
    fresh_rows = q_heads.shape[0]
    factor = q_heads.shape[-1] ** (-0.5)
    all_keys = jnp.concatenate([key_old, key_new], axis=0)
    all_values = jnp.concatenate([value_old, value_new], axis=0)
    scores = (
        jnp.einsum("cgd,kd->gck", q_heads, all_keys, preferred_element_type=jnp.float32) * factor
    )
    key_index = jnp.arange(old_len + fresh_rows, dtype=jnp.int32)[None, :]
    row_index = jnp.arange(fresh_rows, dtype=jnp.int32)[:, None]
    allowed = jnp.where(key_index < old_len, key_index < start_at, key_index - old_len <= row_index)
    scores = jnp.where(allowed[None], scores, NEG)
    row_peak = jnp.max(scores, axis=-1, keepdims=True)
    expd = jnp.exp(scores - row_peak)
    weights = (expd / jnp.sum(expd, axis=-1, keepdims=True)).astype(jnp.bfloat16)
    return jnp.einsum(
        "gck,kd->cgd", weights, all_values, preferred_element_type=jnp.float32
    ).astype(jnp.bfloat16)


def decode_attend(q_heads, key_old, value_old, key_self, value_self, lengths):
    factor = q_heads.shape[-1] ** (-0.5)
    past = jnp.einsum("bgd,bld->bgl", q_heads, key_old, preferred_element_type=jnp.float32) * factor
    slot_index = jnp.arange(key_old.shape[1], dtype=jnp.int32)
    past = jnp.where(slot_index[None, None, :] < lengths[:, None, None], past, NEG)
    own_score = (
        jnp.einsum("bgd,bd->bg", q_heads, key_self, preferred_element_type=jnp.float32) * factor
    )
    row_peak = jnp.maximum(jnp.max(past, axis=-1), own_score)
    past_exp = jnp.exp(past - row_peak[..., None])
    own_exp = jnp.exp(own_score - row_peak)
    row_total = jnp.sum(past_exp, axis=-1) + own_exp
    past_w = (past_exp / row_total[..., None]).astype(jnp.bfloat16)
    own_w = (own_exp / row_total).astype(jnp.bfloat16)
    summed = jnp.einsum("bgl,bld->bgd", past_w, value_old, preferred_element_type=jnp.float32)
    summed = (
        summed + own_w.astype(jnp.float32)[..., None] * value_self.astype(jnp.float32)[:, None, :]
    )
    return summed.astype(jnp.bfloat16)


def butterfly(value, axis, combine):
    size = lax.axis_size(axis)
    step = 1
    while step < size:
        pairs = [(i, i ^ step) for i in range(size)]
        value = combine(value, lax.ppermute(value, axis, pairs))
        step *= 2
    return value


def butterfly_gather(value, axis):
    size = lax.axis_size(axis)
    me = lax.axis_index(axis)
    step = 1
    while step < size:
        pairs = [(i, i ^ step) for i in range(size)]
        other = lax.ppermute(value, axis, pairs)
        low = (me // step) % 2 == 0
        value = jnp.concatenate(
            [jnp.where(low, value, other), jnp.where(low, other, value)], axis=0
        )
        step *= 2
    return value


def regroup(rows_in):
    return lax.all_to_all(rows_in, ("req", "kv"), split_axis=0, concat_axis=0, tiled=True)


def shards(
    hidden_in,
    slot_tokens,
    cache_len,
    prefill_start,
    key_cache,
    value_cache,
    key_prefix,
    value_prefix,
    attn_gain,
    q_proj,
    k_proj,
    v_proj,
    q_gain,
    k_gain,
    o_proj,
    ffn_gain,
    w_gate,
    w_up,
    w_down,
    final_gain,
    lm_head,
):
    req_count = lax.axis_size("req")
    kv_count = lax.axis_size("kv")
    devices = req_count * kv_count
    rows_dev = hidden_in.shape[0]
    kv_index = lax.axis_index("kv")
    self_index = lax.axis_index("req") * kv_count + kv_index
    slot_table = slot_tokens.reshape(devices, rows_dev)
    from_self = slot_table // rows_dev == self_index
    send_rows = jnp.sum(jnp.where(from_self, slot_table - self_index * rows_dev, 0), axis=1)
    slot_place = lax.dynamic_index_in_dim(slot_table, self_index, 0, keepdims=False) // rows_dev
    arrived = regroup(hidden_in[send_rows])
    owner_rows = arrived[slot_place]
    rows_all = lax.all_gather(owner_rows, "kv", axis=0, tiled=True)
    normed = norm_rows(rows_all, attn_gain).astype(jnp.bfloat16)
    o_full = lax.all_to_all(
        jnp.broadcast_to(o_proj[None], (kv_count,) + o_proj.shape), "kv", split_axis=0, concat_axis=0, tiled=True
    ).reshape(kv_count * o_proj.shape[0], o_proj.shape[1])
    ff_dev = w_gate.shape[1]
    ff_piece = ff_dev // kv_count
    weight_piece = jnp.stack(
        [
            lax.dynamic_slice_in_dim(w_gate, kv_index * ff_piece, ff_piece, axis=1).T,
            lax.dynamic_slice_in_dim(w_up, kv_index * ff_piece, ff_piece, axis=1).T,
        ]
    )
    weight_all = lax.all_gather(weight_piece, "req", axis=1, tiled=True)
    down_piece = lax.dynamic_slice_in_dim(w_down, kv_index * ff_piece, ff_piece, axis=0)
    down_all = lax.all_to_all(
        jnp.broadcast_to(down_piece[None], (req_count,) + down_piece.shape),
        "req",
        split_axis=0,
        concat_axis=0,
        tiled=True,
    )
    model_dim = w_gate.shape[0]
    q_cols = q_proj.shape[1]
    kv_cols = k_proj.shape[1]
    projected = jnp.concatenate(
        [
            jnp.dot(normed, q_proj, preferred_element_type=jnp.float32),
            jnp.dot(normed, k_proj, preferred_element_type=jnp.float32),
            jnp.dot(normed, v_proj, preferred_element_type=jnp.float32),
        ],
        axis=1,
    )
    tok_req = projected.shape[0]
    head_dim = q_gain.shape[0]
    dec_count = cache_len.shape[0]
    fresh_count = tok_req - dec_count
    q_raw = projected[:, :q_cols].reshape(tok_req, q_cols // head_dim, head_dim)
    k_raw = projected[:, q_cols : q_cols + kv_cols].reshape(tok_req, kv_cols // head_dim, head_dim)
    v_new = (
        projected[:, q_cols + kv_cols :]
        .astype(jnp.bfloat16)
        .reshape(tok_req, kv_cols // head_dim, head_dim)
    )
    places = jnp.concatenate(
        [prefill_start[0] + jnp.arange(fresh_count, dtype=jnp.int32), cache_len]
    ).astype(jnp.float32)
    queries = rotate(norm_rows(q_raw, q_gain), places).astype(jnp.bfloat16)
    keys_new = rotate(norm_rows(k_raw, k_gain), places).astype(jnp.bfloat16)
    pre_out = prefill_full(
        queries[:fresh_count],
        key_prefix[0, :, 0:head_dim],
        value_prefix[0, :, 0:head_dim],
        keys_new[:fresh_count, 0],
        v_new[:fresh_count, 0],
        prefill_start[0],
    )
    dec_out = decode_attend(
        queries[fresh_count:],
        key_cache,
        value_cache,
        keys_new[fresh_count:, 0],
        v_new[fresh_count:, 0],
        cache_len,
    )
    pieces = jnp.concatenate([pre_out, dec_out], axis=0)
    pieces, weight_all, down_all, o_full = lax.optimization_barrier((pieces, weight_all, down_all, o_full))
    gate_w = weight_all[0]
    up_w = weight_all[1]
    down_w = down_all.reshape(req_count * ff_piece, model_dim)
    attended = lax.all_gather(pieces.reshape(tok_req, q_cols), "kv", axis=1, tiled=True)
    resid = (
        rows_all.astype(jnp.float32) + jnp.dot(attended, o_full, preferred_element_type=jnp.float32)
    ).astype(jnp.bfloat16)
    ffn_in = norm_rows(resid, ffn_gain).astype(jnp.bfloat16)
    contract_last = (((1,), (1,)), ((), ()))
    gate_part = lax.dot_general(ffn_in, gate_w, contract_last, preferred_element_type=jnp.float32)
    up_part = lax.dot_general(ffn_in, up_w, contract_last, preferred_element_type=jnp.float32)
    hidden_act = (jax.nn.silu(gate_part) * up_part).astype(jnp.bfloat16)
    tail_count = tok_req - fresh_count + 1
    tail_pad = -(-tail_count // 8) * 8
    down_part = jnp.dot(hidden_act, down_w, preferred_element_type=jnp.float32)
    ffn_part = lax.psum_scatter(down_part, "kv", scatter_dimension=0, tiled=True)
    tail_part = jnp.dot(hidden_act[tok_req - tail_pad :], down_w, preferred_element_type=jnp.float32)
    tail_sum = butterfly(tail_part, "kv", jnp.add)[tail_pad - tail_count :]
    tail_out = (resid[fresh_count - 1 :].astype(jnp.float32) + tail_sum).astype(jnp.bfloat16)
    tail_rows = norm_rows(tail_out, final_gain).astype(jnp.bfloat16)
    local_peaks = jnp.max(
        jnp.dot(
            butterfly_gather(tail_rows, "req"),
            lm_head,
            preferred_element_type=jnp.float32,
        ),
        axis=1,
    )
    max_logit = butterfly(butterfly(local_peaks, "kv", jnp.maximum), "req", jnp.maximum)
    ffn_part, max_logit = lax.optimization_barrier((ffn_part, max_logit))
    mine = lax.dynamic_slice_in_dim(resid, kv_index * rows_dev, rows_dev, axis=0)
    out_rows = (mine.astype(jnp.float32) + ffn_part).astype(jnp.bfloat16)
    going_back = jnp.zeros_like(out_rows).at[slot_place].set(out_rows)
    returned = regroup(going_back)
    layer_out = jnp.zeros_like(hidden_in).at[send_rows].set(returned)
    return (layer_out, max_logit)


def solution(mesh):
    placed = (
        P(("req", "kv"), None),
        P(),
        P("req"),
        P("req"),
        P("req", None, "kv"),
        P("req", None, "kv"),
        P("req", None, "kv"),
        P("req", None, "kv"),
        P(),
        P(None, "kv"),
        P(None, "kv"),
        P(None, "kv"),
        P(),
        P(),
        P("kv", None),
        P(),
        P(None, "req"),
        P(None, "req"),
        P("req", None),
        P(),
        P(None, ("req", "kv")),
    )
    return jax.shard_map(
        shards, mesh=mesh, in_specs=placed, out_specs=(P(("req", "kv"), None), P()), check_vma=False
    )
```

```python
import jax
import jax.numpy as jnp
from jax import lax
from jax.sharding import PartitionSpec as P

EPS = 1e-06
NEG = -1e30


def spread(value, axis, root):
    mine = lax.axis_index(axis) == root
    return lax.psum(jnp.where(mine, value, jnp.zeros_like(value)), axis)


def norm_rows(values, gain_vec):
    wide = values.astype(jnp.float32)
    return wide * lax.rsqrt(jnp.mean(wide * wide, axis=-1, keepdims=True) + EPS) * gain_vec


def rotate(values, places):
    half_dim = values.shape[-1] // 2
    freqs = 1000000.0 ** (-(jnp.arange(half_dim, dtype=jnp.float32) * 2.0 / values.shape[-1]))
    angles = places[:, None] * freqs[None, :]
    cosine = jnp.cos(angles)[:, None, :]
    sine = jnp.sin(angles)[:, None, :]
    first_half = values[..., :half_dim]
    second_half = values[..., half_dim:]
    return jnp.concatenate(
        [first_half * cosine - second_half * sine, second_half * cosine + first_half * sine],
        axis=-1,
    )


def prefill_full(q_heads, key_old, value_old, key_new, value_new, start_at):
    old_len = key_old.shape[0]
    fresh_rows = q_heads.shape[0]
    factor = q_heads.shape[-1] ** (-0.5)
    all_keys = jnp.concatenate([key_old, key_new], axis=0)
    all_values = jnp.concatenate([value_old, value_new], axis=0)
    scores = (
        jnp.einsum("cgd,kd->gck", q_heads, all_keys, preferred_element_type=jnp.float32) * factor
    )
    key_index = jnp.arange(old_len + fresh_rows, dtype=jnp.int32)[None, :]
    row_index = jnp.arange(fresh_rows, dtype=jnp.int32)[:, None]
    allowed = jnp.where(key_index < old_len, key_index < start_at, key_index - old_len <= row_index)
    scores = jnp.where(allowed[None], scores, NEG)
    row_peak = jnp.max(scores, axis=-1, keepdims=True)
    expd = jnp.exp(scores - row_peak)
    weights = (expd / jnp.sum(expd, axis=-1, keepdims=True)).astype(jnp.bfloat16)
    return jnp.einsum(
        "gck,kd->cgd", weights, all_values, preferred_element_type=jnp.float32
    ).astype(jnp.bfloat16)


def decode_attend(q_heads, key_old, value_old, key_self, value_self, lengths):
    factor = q_heads.shape[-1] ** (-0.5)
    past = jnp.einsum("bgd,bld->bgl", q_heads, key_old, preferred_element_type=jnp.float32) * factor
    slot_index = jnp.arange(key_old.shape[1], dtype=jnp.int32)
    past = jnp.where(slot_index[None, None, :] < lengths[:, None, None], past, NEG)
    own_score = (
        jnp.einsum("bgd,bd->bg", q_heads, key_self, preferred_element_type=jnp.float32) * factor
    )
    row_peak = jnp.maximum(jnp.max(past, axis=-1), own_score)
    past_exp = jnp.exp(past - row_peak[..., None])
    own_exp = jnp.exp(own_score - row_peak)
    row_total = jnp.sum(past_exp, axis=-1) + own_exp
    past_w = (past_exp / row_total[..., None]).astype(jnp.bfloat16)
    own_w = (own_exp / row_total).astype(jnp.bfloat16)
    summed = jnp.einsum("bgl,bld->bgd", past_w, value_old, preferred_element_type=jnp.float32)
    summed = (
        summed + own_w.astype(jnp.float32)[..., None] * value_self.astype(jnp.float32)[:, None, :]
    )
    return summed.astype(jnp.bfloat16)


def butterfly(value, axis, combine):
    size = lax.axis_size(axis)
    step = 1
    while step < size:
        pairs = [(i, i ^ step) for i in range(size)]
        value = combine(value, lax.ppermute(value, axis, pairs))
        step *= 2
    return value


def butterfly_gather(value, axis):
    size = lax.axis_size(axis)
    me = lax.axis_index(axis)
    step = 1
    while step < size:
        pairs = [(i, i ^ step) for i in range(size)]
        other = lax.ppermute(value, axis, pairs)
        low = (me // step) % 2 == 0
        value = jnp.concatenate(
            [jnp.where(low, value, other), jnp.where(low, other, value)], axis=0
        )
        step *= 2
    return value


def radix_exchange(value, axis, step, radix):
    size = lax.axis_size(axis)
    got = [value]
    for digit in range(1, radix):
        pairs = [(i, i ^ (digit * step)) for i in range(size)]
        got.append(lax.ppermute(value, axis, pairs))
    return got


def radix_reduce(value, axis, combine, radix):
    size = lax.axis_size(axis)
    step = 1
    while step < size:
        for other in radix_exchange(value, axis, step, radix)[1:]:
            value = combine(value, other)
        step *= radix
    return value


def radix_gather(value, axis, radix):
    size = lax.axis_size(axis)
    me = lax.axis_index(axis)
    step = 1
    while step < size:
        got = radix_exchange(value, axis, step, radix)
        order = jnp.arange(radix, dtype=jnp.int32) ^ ((me // step) % radix)
        value = jnp.stack(got)[order].reshape((radix * value.shape[0],) + value.shape[1:])
        step *= radix
    return value


def regroup(rows_in):
    return lax.all_to_all(rows_in, ("req", "kv"), split_axis=0, concat_axis=0, tiled=True)


def shards(
    hidden_in,
    slot_tokens,
    cache_len,
    prefill_start,
    key_cache,
    value_cache,
    key_prefix,
    value_prefix,
    attn_gain,
    q_proj,
    k_proj,
    v_proj,
    q_gain,
    k_gain,
    o_proj,
    ffn_gain,
    w_gate,
    w_up,
    w_down,
    final_gain,
    lm_head,
):
    req_count = lax.axis_size("req")
    kv_count = lax.axis_size("kv")
    devices = req_count * kv_count
    rows_dev = hidden_in.shape[0]
    kv_index = lax.axis_index("kv")
    self_index = lax.axis_index("req") * kv_count + kv_index
    slot_table = slot_tokens.reshape(devices, rows_dev)
    from_self = slot_table // rows_dev == self_index
    send_rows = jnp.sum(jnp.where(from_self, slot_table - self_index * rows_dev, 0), axis=1)
    slot_place = lax.dynamic_index_in_dim(slot_table, self_index, 0, keepdims=False) // rows_dev
    arrived = regroup(hidden_in[send_rows])
    owner_rows = arrived[slot_place]
    rows_all = lax.all_gather(owner_rows, "kv", axis=0, tiled=True)
    normed = norm_rows(rows_all, attn_gain).astype(jnp.bfloat16)
    o_full = lax.all_to_all(
        jnp.broadcast_to(o_proj[None], (kv_count,) + o_proj.shape), "kv", split_axis=0, concat_axis=0, tiled=True
    ).reshape(kv_count * o_proj.shape[0], o_proj.shape[1])
    ff_dev = w_gate.shape[1]
    ff_piece = ff_dev // kv_count
    weight_piece = jnp.stack(
        [
            lax.dynamic_slice_in_dim(w_gate, kv_index * ff_piece, ff_piece, axis=1).T,
            lax.dynamic_slice_in_dim(w_up, kv_index * ff_piece, ff_piece, axis=1).T,
            lax.dynamic_slice_in_dim(w_down, kv_index * ff_piece, ff_piece, axis=0),
        ]
    )
    weight_all = lax.all_gather(weight_piece, "req", axis=1, tiled=True)
    model_dim = w_gate.shape[0]
    q_cols = q_proj.shape[1]
    kv_cols = k_proj.shape[1]
    projected = jnp.concatenate(
        [
            jnp.dot(normed, q_proj, preferred_element_type=jnp.float32),
            jnp.dot(normed, k_proj, preferred_element_type=jnp.float32),
            jnp.dot(normed, v_proj, preferred_element_type=jnp.float32),
        ],
        axis=1,
    )
    tok_req = projected.shape[0]
    head_dim = q_gain.shape[0]
    dec_count = cache_len.shape[0]
    fresh_count = tok_req - dec_count
    q_raw = projected[:, :q_cols].reshape(tok_req, q_cols // head_dim, head_dim)
    k_raw = projected[:, q_cols : q_cols + kv_cols].reshape(tok_req, kv_cols // head_dim, head_dim)
    v_new = (
        projected[:, q_cols + kv_cols :]
        .astype(jnp.bfloat16)
        .reshape(tok_req, kv_cols // head_dim, head_dim)
    )
    places = jnp.concatenate(
        [prefill_start[0] + jnp.arange(fresh_count, dtype=jnp.int32), cache_len]
    ).astype(jnp.float32)
    queries = rotate(norm_rows(q_raw, q_gain), places).astype(jnp.bfloat16)
    keys_new = rotate(norm_rows(k_raw, k_gain), places).astype(jnp.bfloat16)
    pre_out = prefill_full(
        queries[:fresh_count],
        key_prefix[0, :, 0:head_dim],
        value_prefix[0, :, 0:head_dim],
        keys_new[:fresh_count, 0],
        v_new[:fresh_count, 0],
        prefill_start[0],
    )
    dec_out = decode_attend(
        queries[fresh_count:],
        key_cache,
        value_cache,
        keys_new[fresh_count:, 0],
        v_new[fresh_count:, 0],
        cache_len,
    )
    pieces = jnp.concatenate([pre_out, dec_out], axis=0)
    pieces, weight_all, o_full = lax.optimization_barrier((pieces, weight_all, o_full))
    gate_w = weight_all[0]
    up_w = weight_all[1]
    down_w = weight_all[2]
    attended = lax.all_gather(pieces.reshape(tok_req, q_cols), "kv", axis=1, tiled=True)
    resid = (
        rows_all.astype(jnp.float32) + jnp.dot(attended, o_full, preferred_element_type=jnp.float32)
    ).astype(jnp.bfloat16)
    ffn_in = norm_rows(resid, ffn_gain).astype(jnp.bfloat16)
    contract_last = (((1,), (1,)), ((), ()))
    gate_part = lax.dot_general(ffn_in, gate_w, contract_last, preferred_element_type=jnp.float32)
    up_part = lax.dot_general(ffn_in, up_w, contract_last, preferred_element_type=jnp.float32)
    hidden_act = (jax.nn.silu(gate_part) * up_part).astype(jnp.bfloat16)
    tail_count = tok_req - fresh_count + 1
    tail_pad = -(-tail_count // 8) * 8
    down_part = jnp.dot(hidden_act, down_w, preferred_element_type=jnp.float32)
    ffn_part = lax.psum_scatter(down_part, "kv", scatter_dimension=0, tiled=True)
    tail_part = jnp.dot(hidden_act[tok_req - tail_pad :], down_w, preferred_element_type=jnp.float32)
    tail_sum = butterfly(tail_part, "kv", jnp.add)[tail_pad - tail_count :]
    tail_out = (resid[fresh_count - 1 :].astype(jnp.float32) + tail_sum).astype(jnp.bfloat16)
    tail_rows = norm_rows(tail_out, final_gain).astype(jnp.bfloat16)
    local_peaks = jnp.max(
        jnp.dot(
            radix_gather(tail_rows, "req", 4),
            lm_head,
            preferred_element_type=jnp.float32,
        ),
        axis=1,
    )
    max_logit = radix_reduce(butterfly(local_peaks, "kv", jnp.maximum), "req", jnp.maximum, 4)
    ffn_part, max_logit = lax.optimization_barrier((ffn_part, max_logit))
    mine = lax.dynamic_slice_in_dim(resid, kv_index * rows_dev, rows_dev, axis=0)
    out_rows = (mine.astype(jnp.float32) + ffn_part).astype(jnp.bfloat16)
    going_back = jnp.zeros_like(out_rows).at[slot_place].set(out_rows)
    returned = regroup(going_back)
    layer_out = jnp.zeros_like(hidden_in).at[send_rows].set(returned)
    return (layer_out, max_logit)


def solution(mesh):
    placed = (
        P(("req", "kv"), None),
        P(),
        P("req"),
        P("req"),
        P("req", None, "kv"),
        P("req", None, "kv"),
        P("req", None, "kv"),
        P("req", None, "kv"),
        P(),
        P(None, "kv"),
        P(None, "kv"),
        P(None, "kv"),
        P(),
        P(),
        P("kv", None),
        P(),
        P(None, "req"),
        P(None, "req"),
        P("req", None),
        P(),
        P(None, ("req", "kv")),
    )
    return jax.shard_map(
        shards, mesh=mesh, in_specs=placed, out_specs=(P(("req", "kv"), None), P()), check_vma=False
    )
```

```python
import jax
import jax.numpy as jnp
from jax import lax
from jax.sharding import PartitionSpec as P

EPS = 1e-06
NEG = -1e30


def spread(value, axis, root):
    mine = lax.axis_index(axis) == root
    return lax.psum(jnp.where(mine, value, jnp.zeros_like(value)), axis)


def norm_rows(values, gain_vec):
    wide = values.astype(jnp.float32)
    return wide * lax.rsqrt(jnp.mean(wide * wide, axis=-1, keepdims=True) + EPS) * gain_vec


def rotate(values, places):
    half_dim = values.shape[-1] // 2
    freqs = 1000000.0 ** (-(jnp.arange(half_dim, dtype=jnp.float32) * 2.0 / values.shape[-1]))
    angles = places[:, None] * freqs[None, :]
    cosine = jnp.cos(angles)[:, None, :]
    sine = jnp.sin(angles)[:, None, :]
    first_half = values[..., :half_dim]
    second_half = values[..., half_dim:]
    return jnp.concatenate(
        [first_half * cosine - second_half * sine, second_half * cosine + first_half * sine],
        axis=-1,
    )


def prefill_full(q_heads, key_old, value_old, key_new, value_new, start_at):
    old_len = key_old.shape[0]
    fresh_rows = q_heads.shape[0]
    factor = q_heads.shape[-1] ** (-0.5)
    all_keys = jnp.concatenate([key_old, key_new], axis=0)
    all_values = jnp.concatenate([value_old, value_new], axis=0)
    scores = (
        jnp.einsum("cgd,kd->gck", q_heads, all_keys, preferred_element_type=jnp.float32) * factor
    )
    key_index = jnp.arange(old_len + fresh_rows, dtype=jnp.int32)[None, :]
    row_index = jnp.arange(fresh_rows, dtype=jnp.int32)[:, None]
    allowed = jnp.where(key_index < old_len, key_index < start_at, key_index - old_len <= row_index)
    scores = jnp.where(allowed[None], scores, NEG)
    row_peak = jnp.max(scores, axis=-1, keepdims=True)
    expd = jnp.exp(scores - row_peak)
    weights = (expd / jnp.sum(expd, axis=-1, keepdims=True)).astype(jnp.bfloat16)
    return jnp.einsum(
        "gck,kd->cgd", weights, all_values, preferred_element_type=jnp.float32
    ).astype(jnp.bfloat16)


def decode_attend(q_heads, key_old, value_old, key_self, value_self, lengths):
    factor = q_heads.shape[-1] ** (-0.5)
    past = jnp.einsum("bgd,bld->bgl", q_heads, key_old, preferred_element_type=jnp.float32) * factor
    slot_index = jnp.arange(key_old.shape[1], dtype=jnp.int32)
    past = jnp.where(slot_index[None, None, :] < lengths[:, None, None], past, NEG)
    own_score = (
        jnp.einsum("bgd,bd->bg", q_heads, key_self, preferred_element_type=jnp.float32) * factor
    )
    row_peak = jnp.maximum(jnp.max(past, axis=-1), own_score)
    past_exp = jnp.exp(past - row_peak[..., None])
    own_exp = jnp.exp(own_score - row_peak)
    row_total = jnp.sum(past_exp, axis=-1) + own_exp
    past_w = (past_exp / row_total[..., None]).astype(jnp.bfloat16)
    own_w = (own_exp / row_total).astype(jnp.bfloat16)
    summed = jnp.einsum("bgl,bld->bgd", past_w, value_old, preferred_element_type=jnp.float32)
    summed = (
        summed + own_w.astype(jnp.float32)[..., None] * value_self.astype(jnp.float32)[:, None, :]
    )
    return summed.astype(jnp.bfloat16)


def butterfly(value, axis, combine):
    size = lax.axis_size(axis)
    step = 1
    while step < size:
        pairs = [(i, i ^ step) for i in range(size)]
        value = combine(value, lax.ppermute(value, axis, pairs))
        step *= 2
    return value


def butterfly_gather(value, axis):
    size = lax.axis_size(axis)
    me = lax.axis_index(axis)
    step = 1
    while step < size:
        pairs = [(i, i ^ step) for i in range(size)]
        other = lax.ppermute(value, axis, pairs)
        low = (me // step) % 2 == 0
        value = jnp.concatenate(
            [jnp.where(low, value, other), jnp.where(low, other, value)], axis=0
        )
        step *= 2
    return value


def radix_exchange(value, axis, step, radix):
    size = lax.axis_size(axis)
    got = [value]
    for digit in range(1, radix):
        pairs = [(i, i ^ (digit * step)) for i in range(size)]
        got.append(lax.ppermute(value, axis, pairs))
    return got


def radix_reduce(value, axis, combine, radix):
    size = lax.axis_size(axis)
    step = 1
    while step < size:
        for other in radix_exchange(value, axis, step, radix)[1:]:
            value = combine(value, other)
        step *= radix
    return value


def radix_gather(value, axis, radix):
    size = lax.axis_size(axis)
    me = lax.axis_index(axis)
    step = 1
    while step < size:
        got = radix_exchange(value, axis, step, radix)
        order = jnp.arange(radix, dtype=jnp.int32) ^ ((me // step) % radix)
        value = jnp.stack(got)[order].reshape((radix * value.shape[0],) + value.shape[1:])
        step *= radix
    return value


def mixed_reduce(value, axis, combine, radices):
    me = lax.axis_index(axis)
    step = 1
    for radix in radices:
        got = radix_exchange(value, axis, step, radix)
        order = jnp.arange(radix, dtype=jnp.int32) ^ ((me // step) % radix)
        members = jnp.stack(got)[order]
        while members.shape[0] > 1:
            members = combine(members[0::2], members[1::2])
        value = members[0]
        step *= radix
    return value


def regroup(rows_in):
    return lax.all_to_all(rows_in, ("req", "kv"), split_axis=0, concat_axis=0, tiled=True)


def shards(
    hidden_in,
    slot_tokens,
    cache_len,
    prefill_start,
    key_cache,
    value_cache,
    key_prefix,
    value_prefix,
    attn_gain,
    q_proj,
    k_proj,
    v_proj,
    q_gain,
    k_gain,
    o_proj,
    ffn_gain,
    w_gate,
    w_up,
    w_down,
    final_gain,
    lm_head,
):
    req_count = lax.axis_size("req")
    kv_count = lax.axis_size("kv")
    devices = req_count * kv_count
    rows_dev = hidden_in.shape[0]
    kv_index = lax.axis_index("kv")
    self_index = lax.axis_index("req") * kv_count + kv_index
    slot_table = slot_tokens.reshape(devices, rows_dev)
    from_self = slot_table // rows_dev == self_index
    send_rows = jnp.sum(jnp.where(from_self, slot_table - self_index * rows_dev, 0), axis=1)
    slot_place = lax.dynamic_index_in_dim(slot_table, self_index, 0, keepdims=False) // rows_dev
    arrived = regroup(hidden_in[send_rows])
    owner_rows = arrived[slot_place]
    rows_all = lax.all_gather(owner_rows, "kv", axis=0, tiled=True)
    normed = norm_rows(rows_all, attn_gain).astype(jnp.bfloat16)
    o_full = lax.all_to_all(
        jnp.broadcast_to(o_proj[None], (kv_count,) + o_proj.shape), "kv", split_axis=0, concat_axis=0, tiled=True
    ).reshape(kv_count * o_proj.shape[0], o_proj.shape[1])
    ff_dev = w_gate.shape[1]
    ff_piece = ff_dev // kv_count
    weight_piece = jnp.stack(
        [
            lax.dynamic_slice_in_dim(w_gate, kv_index * ff_piece, ff_piece, axis=1).T,
            lax.dynamic_slice_in_dim(w_up, kv_index * ff_piece, ff_piece, axis=1).T,
            lax.dynamic_slice_in_dim(w_down, kv_index * ff_piece, ff_piece, axis=0),
        ]
    )
    weight_all = lax.all_gather(weight_piece, "req", axis=1, tiled=True)
    model_dim = w_gate.shape[0]
    q_cols = q_proj.shape[1]
    kv_cols = k_proj.shape[1]
    projected = jnp.concatenate(
        [
            jnp.dot(normed, q_proj, preferred_element_type=jnp.float32),
            jnp.dot(normed, k_proj, preferred_element_type=jnp.float32),
            jnp.dot(normed, v_proj, preferred_element_type=jnp.float32),
        ],
        axis=1,
    )
    tok_req = projected.shape[0]
    head_dim = q_gain.shape[0]
    dec_count = cache_len.shape[0]
    fresh_count = tok_req - dec_count
    q_raw = projected[:, :q_cols].reshape(tok_req, q_cols // head_dim, head_dim)
    k_raw = projected[:, q_cols : q_cols + kv_cols].reshape(tok_req, kv_cols // head_dim, head_dim)
    v_new = (
        projected[:, q_cols + kv_cols :]
        .astype(jnp.bfloat16)
        .reshape(tok_req, kv_cols // head_dim, head_dim)
    )
    places = jnp.concatenate(
        [prefill_start[0] + jnp.arange(fresh_count, dtype=jnp.int32), cache_len]
    ).astype(jnp.float32)
    queries = rotate(norm_rows(q_raw, q_gain), places).astype(jnp.bfloat16)
    keys_new = rotate(norm_rows(k_raw, k_gain), places).astype(jnp.bfloat16)
    pre_out = prefill_full(
        queries[:fresh_count],
        key_prefix[0, :, 0:head_dim],
        value_prefix[0, :, 0:head_dim],
        keys_new[:fresh_count, 0],
        v_new[:fresh_count, 0],
        prefill_start[0],
    )
    dec_out = decode_attend(
        queries[fresh_count:],
        key_cache,
        value_cache,
        keys_new[fresh_count:, 0],
        v_new[fresh_count:, 0],
        cache_len,
    )
    pieces = jnp.concatenate([pre_out, dec_out], axis=0)
    pieces, weight_all, o_full = lax.optimization_barrier((pieces, weight_all, o_full))
    gate_w = weight_all[0]
    up_w = weight_all[1]
    down_w = weight_all[2]
    attended = lax.all_gather(pieces.reshape(tok_req, q_cols), "kv", axis=1, tiled=True)
    resid = (
        rows_all.astype(jnp.float32) + jnp.dot(attended, o_full, preferred_element_type=jnp.float32)
    ).astype(jnp.bfloat16)
    ffn_in = norm_rows(resid, ffn_gain).astype(jnp.bfloat16)
    contract_last = (((1,), (1,)), ((), ()))
    gate_part = lax.dot_general(ffn_in, gate_w, contract_last, preferred_element_type=jnp.float32)
    up_part = lax.dot_general(ffn_in, up_w, contract_last, preferred_element_type=jnp.float32)
    hidden_act = (jax.nn.silu(gate_part) * up_part).astype(jnp.bfloat16)
    tail_count = tok_req - fresh_count + 1
    tail_pad = -(-tail_count // 8) * 8
    down_part = jnp.dot(hidden_act, down_w, preferred_element_type=jnp.float32)
    ffn_part = lax.psum_scatter(down_part, "kv", scatter_dimension=0, tiled=True)
    tail_part = jnp.dot(hidden_act[tok_req - tail_pad :], down_w, preferred_element_type=jnp.float32)
    tail_sum = mixed_reduce(tail_part, "kv", jnp.add, (2, 4))[tail_pad - tail_count :]
    tail_out = (resid[fresh_count - 1 :].astype(jnp.float32) + tail_sum).astype(jnp.bfloat16)
    tail_rows = norm_rows(tail_out, final_gain).astype(jnp.bfloat16)
    local_peaks = jnp.max(
        jnp.dot(
            radix_gather(tail_rows, "req", 4),
            lm_head,
            preferred_element_type=jnp.float32,
        ),
        axis=1,
    )
    max_logit = radix_reduce(mixed_reduce(local_peaks, "kv", jnp.maximum, (2, 4)), "req", jnp.maximum, 4)
    ffn_part, max_logit = lax.optimization_barrier((ffn_part, max_logit))
    mine = lax.dynamic_slice_in_dim(resid, kv_index * rows_dev, rows_dev, axis=0)
    out_rows = (mine.astype(jnp.float32) + ffn_part).astype(jnp.bfloat16)
    going_back = jnp.zeros_like(out_rows).at[slot_place].set(out_rows)
    returned = regroup(going_back)
    layer_out = jnp.zeros_like(hidden_in).at[send_rows].set(returned)
    return (layer_out, max_logit)


def solution(mesh):
    placed = (
        P(("req", "kv"), None),
        P(),
        P("req"),
        P("req"),
        P("req", None, "kv"),
        P("req", None, "kv"),
        P("req", None, "kv"),
        P("req", None, "kv"),
        P(),
        P(None, "kv"),
        P(None, "kv"),
        P(None, "kv"),
        P(),
        P(),
        P("kv", None),
        P(),
        P(None, "req"),
        P(None, "req"),
        P("req", None),
        P(),
        P(None, ("req", "kv")),
    )
    return jax.shard_map(
        shards, mesh=mesh, in_specs=placed, out_specs=(P(("req", "kv"), None), P()), check_vma=False
    )
```

```python
import jax
import jax.numpy as jnp
from jax import lax
from jax.sharding import PartitionSpec as P

EPS = 1e-06
NEG = -1e30


def spread(value, axis, root):
    mine = lax.axis_index(axis) == root
    return lax.psum(jnp.where(mine, value, jnp.zeros_like(value)), axis)


def norm_rows(values, gain_vec):
    wide = values.astype(jnp.float32)
    return wide * lax.rsqrt(jnp.mean(wide * wide, axis=-1, keepdims=True) + EPS) * gain_vec


def rotate(values, places):
    half_dim = values.shape[-1] // 2
    freqs = 1000000.0 ** (-(jnp.arange(half_dim, dtype=jnp.float32) * 2.0 / values.shape[-1]))
    angles = places[:, None] * freqs[None, :]
    cosine = jnp.cos(angles)[:, None, :]
    sine = jnp.sin(angles)[:, None, :]
    first_half = values[..., :half_dim]
    second_half = values[..., half_dim:]
    return jnp.concatenate(
        [first_half * cosine - second_half * sine, second_half * cosine + first_half * sine],
        axis=-1,
    )


def prefill_full(q_heads, key_old, value_old, key_new, value_new, start_at):
    old_len = key_old.shape[0]
    fresh_rows = q_heads.shape[0]
    factor = q_heads.shape[-1] ** (-0.5)
    all_keys = jnp.concatenate([key_old, key_new], axis=0)
    all_values = jnp.concatenate([value_old, value_new], axis=0)
    scores = (
        jnp.einsum("cgd,kd->gck", q_heads, all_keys, preferred_element_type=jnp.float32) * factor
    )
    key_index = jnp.arange(old_len + fresh_rows, dtype=jnp.int32)[None, :]
    row_index = jnp.arange(fresh_rows, dtype=jnp.int32)[:, None]
    allowed = jnp.where(key_index < old_len, key_index < start_at, key_index - old_len <= row_index)
    scores = jnp.where(allowed[None], scores, NEG)
    row_peak = jnp.max(scores, axis=-1, keepdims=True)
    expd = jnp.exp(scores - row_peak)
    weights = (expd / jnp.sum(expd, axis=-1, keepdims=True)).astype(jnp.bfloat16)
    return jnp.einsum(
        "gck,kd->cgd", weights, all_values, preferred_element_type=jnp.float32
    ).astype(jnp.bfloat16)


def decode_attend(q_heads, key_old, value_old, key_self, value_self, lengths):
    factor = q_heads.shape[-1] ** (-0.5)
    past = jnp.einsum("bgd,bld->bgl", q_heads, key_old, preferred_element_type=jnp.float32) * factor
    slot_index = jnp.arange(key_old.shape[1], dtype=jnp.int32)
    past = jnp.where(slot_index[None, None, :] < lengths[:, None, None], past, NEG)
    own_score = (
        jnp.einsum("bgd,bd->bg", q_heads, key_self, preferred_element_type=jnp.float32) * factor
    )
    row_peak = jnp.maximum(jnp.max(past, axis=-1), own_score)
    past_exp = jnp.exp(past - row_peak[..., None])
    own_exp = jnp.exp(own_score - row_peak)
    row_total = jnp.sum(past_exp, axis=-1) + own_exp
    past_w = (past_exp / row_total[..., None]).astype(jnp.bfloat16)
    own_w = (own_exp / row_total).astype(jnp.bfloat16)
    summed = jnp.einsum("bgl,bld->bgd", past_w, value_old, preferred_element_type=jnp.float32)
    summed = (
        summed + own_w.astype(jnp.float32)[..., None] * value_self.astype(jnp.float32)[:, None, :]
    )
    return summed.astype(jnp.bfloat16)


def butterfly(value, axis, combine):
    size = lax.axis_size(axis)
    step = 1
    while step < size:
        pairs = [(i, i ^ step) for i in range(size)]
        value = combine(value, lax.ppermute(value, axis, pairs))
        step *= 2
    return value


def butterfly_gather(value, axis):
    size = lax.axis_size(axis)
    me = lax.axis_index(axis)
    step = 1
    while step < size:
        pairs = [(i, i ^ step) for i in range(size)]
        other = lax.ppermute(value, axis, pairs)
        low = (me // step) % 2 == 0
        value = jnp.concatenate(
            [jnp.where(low, value, other), jnp.where(low, other, value)], axis=0
        )
        step *= 2
    return value


def radix_exchange(value, axis, step, radix):
    size = lax.axis_size(axis)
    got = [value]
    for digit in range(1, radix):
        pairs = [(i, i ^ (digit * step)) for i in range(size)]
        got.append(lax.ppermute(value, axis, pairs))
    return got


def radix_reduce(value, axis, combine, radix):
    size = lax.axis_size(axis)
    step = 1
    while step < size:
        for other in radix_exchange(value, axis, step, radix)[1:]:
            value = combine(value, other)
        step *= radix
    return value


def radix_gather(value, axis, radix):
    size = lax.axis_size(axis)
    me = lax.axis_index(axis)
    step = 1
    while step < size:
        got = radix_exchange(value, axis, step, radix)
        order = jnp.arange(radix, dtype=jnp.int32) ^ ((me // step) % radix)
        value = jnp.stack(got)[order].reshape((radix * value.shape[0],) + value.shape[1:])
        step *= radix
    return value


def mixed_reduce(value, axis, combine, radices):
    me = lax.axis_index(axis)
    step = 1
    for radix in radices:
        got = radix_exchange(value, axis, step, radix)
        order = jnp.arange(radix, dtype=jnp.int32) ^ ((me // step) % radix)
        members = jnp.stack(got)[order]
        while members.shape[0] > 1:
            members = combine(members[0::2], members[1::2])
        value = members[0]
        step *= radix
    return value


def regroup(rows_in):
    return lax.all_to_all(rows_in, ("req", "kv"), split_axis=0, concat_axis=0, tiled=True)


def shards(
    hidden_in,
    slot_tokens,
    cache_len,
    prefill_start,
    key_cache,
    value_cache,
    key_prefix,
    value_prefix,
    attn_gain,
    q_proj,
    k_proj,
    v_proj,
    q_gain,
    k_gain,
    o_proj,
    ffn_gain,
    w_gate,
    w_up,
    w_down,
    final_gain,
    lm_head,
):
    req_count = lax.axis_size("req")
    kv_count = lax.axis_size("kv")
    devices = req_count * kv_count
    rows_dev = hidden_in.shape[0]
    kv_index = lax.axis_index("kv")
    self_index = lax.axis_index("req") * kv_count + kv_index
    slot_table = slot_tokens.reshape(devices, rows_dev)
    from_self = slot_table // rows_dev == self_index
    send_rows = jnp.sum(jnp.where(from_self, slot_table - self_index * rows_dev, 0), axis=1)
    slot_place = lax.dynamic_index_in_dim(slot_table, self_index, 0, keepdims=False) // rows_dev
    arrived = regroup(hidden_in[send_rows])
    owner_rows = arrived[slot_place]
    rows_all = lax.all_gather(owner_rows, "kv", axis=0, tiled=True)
    normed = norm_rows(rows_all, attn_gain).astype(jnp.bfloat16)
    o_full = lax.all_to_all(
        jnp.broadcast_to(o_proj[None], (kv_count,) + o_proj.shape), "kv", split_axis=0, concat_axis=0, tiled=True
    ).reshape(kv_count * o_proj.shape[0], o_proj.shape[1])
    ff_dev = w_gate.shape[1]
    ff_piece = ff_dev // kv_count
    weight_piece = jnp.stack(
        [
            lax.dynamic_slice_in_dim(w_gate, kv_index * ff_piece, ff_piece, axis=1).T,
            lax.dynamic_slice_in_dim(w_up, kv_index * ff_piece, ff_piece, axis=1).T,
            lax.dynamic_slice_in_dim(w_down, kv_index * ff_piece, ff_piece, axis=0),
        ]
    )
    weight_all = lax.all_gather(weight_piece, "req", axis=1, tiled=True)
    model_dim = w_gate.shape[0]
    q_cols = q_proj.shape[1]
    kv_cols = k_proj.shape[1]
    projected = jnp.concatenate(
        [
            jnp.dot(normed, q_proj, preferred_element_type=jnp.float32),
            jnp.dot(normed, k_proj, preferred_element_type=jnp.float32),
            jnp.dot(normed, v_proj, preferred_element_type=jnp.float32),
        ],
        axis=1,
    )
    tok_req = projected.shape[0]
    head_dim = q_gain.shape[0]
    dec_count = cache_len.shape[0]
    fresh_count = tok_req - dec_count
    q_raw = projected[:, :q_cols].reshape(tok_req, q_cols // head_dim, head_dim)
    k_raw = projected[:, q_cols : q_cols + kv_cols].reshape(tok_req, kv_cols // head_dim, head_dim)
    v_new = (
        projected[:, q_cols + kv_cols :]
        .astype(jnp.bfloat16)
        .reshape(tok_req, kv_cols // head_dim, head_dim)
    )
    places = jnp.concatenate(
        [prefill_start[0] + jnp.arange(fresh_count, dtype=jnp.int32), cache_len]
    ).astype(jnp.float32)
    queries = rotate(norm_rows(q_raw, q_gain), places).astype(jnp.bfloat16)
    keys_new = rotate(norm_rows(k_raw, k_gain), places).astype(jnp.bfloat16)
    pre_out = prefill_full(
        queries[:fresh_count],
        key_prefix[0, :, 0:head_dim],
        value_prefix[0, :, 0:head_dim],
        keys_new[:fresh_count, 0],
        v_new[:fresh_count, 0],
        prefill_start[0],
    )
    dec_out = decode_attend(
        queries[fresh_count:],
        key_cache,
        value_cache,
        keys_new[fresh_count:, 0],
        v_new[fresh_count:, 0],
        cache_len,
    )
    pieces = jnp.concatenate([pre_out, dec_out], axis=0)
    pieces, weight_all, o_full = lax.optimization_barrier((pieces, weight_all, o_full))
    gate_w = weight_all[0]
    up_w = weight_all[1]
    down_w = weight_all[2]
    attended = lax.all_gather(pieces.reshape(tok_req, q_cols), "kv", axis=1, tiled=True)
    resid = (
        rows_all.astype(jnp.float32) + jnp.dot(attended, o_full, preferred_element_type=jnp.float32)
    ).astype(jnp.bfloat16)
    ffn_in = norm_rows(resid, ffn_gain).astype(jnp.bfloat16)
    contract_last = (((1,), (1,)), ((), ()))
    gate_part = lax.dot_general(ffn_in, gate_w, contract_last, preferred_element_type=jnp.float32)
    up_part = lax.dot_general(ffn_in, up_w, contract_last, preferred_element_type=jnp.float32)
    hidden_act = (jax.nn.silu(gate_part) * up_part).astype(jnp.bfloat16)
    tail_count = tok_req - fresh_count + 1
    tail_pad = -(-tail_count // 8) * 8
    down_part = jnp.dot(hidden_act, down_w, preferred_element_type=jnp.float32)
    ffn_part = lax.psum_scatter(down_part, "kv", scatter_dimension=0, tiled=True)
    tail_part = jnp.dot(hidden_act[tok_req - tail_pad :], down_w, preferred_element_type=jnp.float32)
    tail_sum = mixed_reduce(tail_part, "kv", jnp.add, (2, 4))[tail_pad - tail_count :]
    tail_out = (resid[fresh_count - 1 :].astype(jnp.float32) + tail_sum).astype(jnp.bfloat16)
    tail_rows = norm_rows(tail_out, final_gain).astype(jnp.bfloat16)
    local_peaks = jnp.max(
        jnp.dot(
            radix_gather(tail_rows, "req", 4),
            lm_head,
            preferred_element_type=jnp.float32,
        ),
        axis=1,
    )
    ffn_part, local_peaks = lax.optimization_barrier((ffn_part, local_peaks))
    max_logit = radix_reduce(mixed_reduce(local_peaks, "kv", jnp.maximum, (2, 4)), "req", jnp.maximum, 4)
    mine = lax.dynamic_slice_in_dim(resid, kv_index * rows_dev, rows_dev, axis=0)
    out_rows = (mine.astype(jnp.float32) + ffn_part).astype(jnp.bfloat16)
    going_back = jnp.zeros_like(out_rows).at[slot_place].set(out_rows)
    returned = regroup(going_back)
    layer_out = jnp.zeros_like(hidden_in).at[send_rows].set(returned)
    return (layer_out, max_logit)


def solution(mesh):
    placed = (
        P(("req", "kv"), None),
        P(),
        P("req"),
        P("req"),
        P("req", None, "kv"),
        P("req", None, "kv"),
        P("req", None, "kv"),
        P("req", None, "kv"),
        P(),
        P(None, "kv"),
        P(None, "kv"),
        P(None, "kv"),
        P(),
        P(),
        P("kv", None),
        P(),
        P(None, "req"),
        P(None, "req"),
        P("req", None),
        P(),
        P(None, ("req", "kv")),
    )
    return jax.shard_map(
        shards, mesh=mesh, in_specs=placed, out_specs=(P(("req", "kv"), None), P()), check_vma=False
    )
```
